128 devices in a mesh: seq: 32 (over x, y_lo, z), ch: 4 (over y_hi, core).
Axes of the slice: x: 4, y: 4 (y_hi: 2, y_lo: 2; y = y_hi * 2 + y_lo), z: 4, core: 2. Of those that a mesh axis runs over, the one named last changes fastest.
Arguments:
- query_proj: bfloat16 [4096, 4096], P('seq', 'ch'), may hold values from -6 to 6
- key_proj: bfloat16 [4096, 4096], P('seq', 'ch'), may hold values from -6 to 6
- value_proj: bfloat16 [4096, 4096], P('seq', 'ch'), may hold values from -6 to 6
- feat_weight: float32 [3, 3, 4096], P(None, None, 'ch'), may hold values from -3.5 to 3.5
- long_filter: float32 [4096, 4096], P('seq', 'ch'), may hold values from -2 to 2, as said below
- skip_gain: float32 [4096], P('ch'), may hold values from 0.5 to 1.5
- out_weight: bfloat16 [4096, 4096], P(None, 'ch'), may hold values from -0.09375 to 0.09375
Outputs:
- output: bfloat16 [4096, 4096], P('seq', 'ch')
The draws below stay inside these ranges and needn't reach their ends.
Inputs may be any that keep to these rules, and one draw needn't show every extreme that they name: `long_filter`: taps of the long filters.
All inputs are finite; a program needn't handle non-finite values.
Results may differ from the reference program's by a relative error of at most 0.0049.
Values may be sent and summed in bfloat16 or wider, within the bound.
A program may use at most 128 MiB of HBM per device.

```python
import math
import jax
import jax.numpy as jnp
from jax import lax

D = 4096
TAPS = 3
GROUP = 1
SEQUENCE_TOKENS = 4096
FILTERS = 4096


def draw_long_filter(key, part):
    split_random_keys = jax.random.split(key, 6)
    slow_share = 0.5
    slow_mask = jax.random.bernoulli(split_random_keys[0], slow_share, (FILTERS,))
    slow_rate = math.log(10.0) / (SEQUENCE_TOKENS * jax.random.uniform(split_random_keys[1], (FILTERS,), jnp.float32, 3.0, 6.0))
    fast_rate = math.log(10.0) / jax.random.uniform(split_random_keys[2], (FILTERS,), jnp.float32, 30.0, 50.0)
    decay_rate = jnp.where(slow_mask, slow_rate, fast_rate)
    token_places = jnp.arange(SEQUENCE_TOKENS, dtype=jnp.float32)[:, None]
    decay_envelope = jnp.exp(-decay_rate[None, :] * token_places)
    spike_locations = jax.random.randint(split_random_keys[3], (2,), 1, SEQUENCE_TOKENS)
    spike_dropouts = jax.random.uniform(split_random_keys[4], (2,), jnp.float32, 0.5, 0.8)
    for element_total in range(2):
        decay_envelope = decay_envelope * jnp.where(token_places >= spike_locations[element_total].astype(jnp.float32), spike_dropouts[element_total], 1.0)
    energy = jnp.expm1(-2.0 * decay_rate * SEQUENCE_TOKENS) / jnp.expm1(-2.0 * decay_rate)
    noise_field = jnp.clip(jax.random.normal(split_random_keys[5], (SEQUENCE_TOKENS, FILTERS), jnp.float32), -4.0, 4.0)
    return noise_field * decay_envelope * lax.rsqrt(energy)[None, :]


def steps_of(stream_key, shape, cuts, least, high):
    gain, own = 1.0, jax.random.fold_in(stream_key, 6)
    for dim, shards_of in cuts:
        draws = jnp.exp(jax.random.uniform(jax.random.fold_in(own, dim), (shards_of,), jnp.float32, least / len(cuts), high / len(cuts)))
        gain = gain * jnp.repeat(draws, shape[dim] // shards_of).reshape([-1 if axis == dim else 1 for axis in range(len(shape))])
    return gain


def scatter_about(stream_key, dims, width, limit, cuts=(), kind=jnp.bfloat16):
    entries = width * jax.random.normal(stream_key, dims, jnp.float32)
    if cuts:
        entries = entries * steps_of(stream_key, dims, cuts, -0.22, 0.18)
    return jnp.clip(entries, -limit, limit).astype(kind)


def setup_inputs(seed: int = 0) -> dict:
    key_list = jax.random.split(jax.random.key(seed), 8)
    query_proj = scatter_about(key_list[0], (SEQUENCE_TOKENS, D), 1.0, 6.0, ((0, 32), (1, 4)))
    key_proj = scatter_about(key_list[1], (SEQUENCE_TOKENS, D), 1.0, 6.0, ((0, 32), (1, 4)))
    value_proj = scatter_about(key_list[2], (SEQUENCE_TOKENS, D), 1.0, 6.0, ((0, 32), (1, 4)))
    feat_weight = scatter_about(key_list[3], (3, TAPS, D), TAPS ** -0.5, 3.5, ((2, 4),), jnp.float32)
    long_filter = draw_long_filter(jax.random.fold_in(key_list[7], 71), 0)
    skip_gain = jnp.clip(0.5 + 1.0 * jax.random.uniform(key_list[5], (D,), jnp.float32) ** steps_of(key_list[5], (D,), ((0, 4),), -0.2, 0.2), 0.5, 1.5)
    out_weight = scatter_about(key_list[6], (D, D), D ** -0.5, 0.09375, ((1, 4),))
    return dict(query_proj=query_proj, key_proj=key_proj, value_proj=value_proj, feat_weight=feat_weight, long_filter=long_filter, skip_gain=skip_gain, out_weight=out_weight)


def featurize(signal, tap_weights):
    reach_rows = tap_weights.shape[0] - 1
    row_count = signal.shape[0]
    padded = jnp.pad(signal, ((reach_rows, 0), (0, 0)))
    result = jnp.zeros(signal.shape, jnp.float32)
    for tap_lag in range(reach_rows + 1):
        result = result + tap_weights[tap_lag][None, :] * padded[reach_rows - tap_lag: reach_rows - tap_lag + row_count]
    return result


def reference(query_proj, key_proj, value_proj, feat_weight, long_filter, skip_gain, out_weight):
    query_feat = featurize(query_proj.astype(jnp.float32), feat_weight[0])
    key_feat = featurize(key_proj.astype(jnp.float32), feat_weight[1])
    value_feat = featurize(value_proj.astype(jnp.float32), feat_weight[2])
    gated = key_feat * value_feat
    total_len = 2 * SEQUENCE_TOKENS
    block_width = D // 8
    portions = []
    for block_number in range(8):
        first_col = block_number * block_width
        portion = gated[:, first_col:first_col + block_width]
        spectrum = jnp.fft.rfft(portion, n=total_len, axis=0)
        freq_count = spectrum.shape[0]
        spectrum = spectrum.reshape(freq_count, block_width // GROUP, GROUP)
        filter_part = long_filter[:, first_col // GROUP:(first_col + block_width) // GROUP]
        filter_spec = jnp.fft.rfft(filter_part, n=total_len, axis=0)
        spectrum = spectrum * filter_spec[:, :, None]
        convolved = jnp.fft.irfft(spectrum.reshape(freq_count, block_width), n=total_len, axis=0)[:SEQUENCE_TOKENS]
        portions.append(convolved)
    convolved = jnp.concatenate(portions, axis=1)
    mixed = (query_feat * (convolved + skip_gain[None, :] * gated)).astype(jnp.bfloat16)
    return jnp.dot(mixed, out_weight, preferred_element_type=jnp.float32).astype(jnp.bfloat16)
```

```python
import functools

import jax
import jax.numpy as jnp
import numpy as np
from jax import lax
from jax.experimental import pallas as pl
from jax.experimental.pallas import tpu as pltpu
from jax.sharding import PartitionSpec as P

F32 = jnp.float32
BF16 = jnp.bfloat16
MESH = pl.DeviceIdType.MESH
BLOCKS = 32
LANES = 128
ROWS = 16
HALF_ROOT = float(np.sqrt(0.5))


def tables():
    lane = np.arange(LANES)
    theta = 2 * np.pi * (np.arange(BLOCKS)[:, None] + 0.25) * lane[None, :] / (BLOCKS * LANES)
    twiddle = np.stack([np.cos(theta), np.sin(theta)]).astype(np.float32)
    phase = 2 * np.pi * (lane[:, None] * lane[None, :] % LANES) / LANES
    c, s = np.cos(phase), np.sin(phase)
    forward = np.block([[c, -s], [s, c]])
    inverse = np.block([[c, s], [-s, c]]) / (BLOCKS * LANES)
    parts = []
    for matrix in (forward, inverse):
        high = matrix.astype(BF16)
        parts += [high, (matrix - high.astype(np.float64)).astype(BF16)]
    return jnp.asarray(twiddle), jnp.asarray(np.stack(parts))


def times(value, angle):
    re, im = value
    c, s = float(np.cos(angle)), float(np.sin(angle))
    if abs(angle) < 1e-12:
        return re, im
    return re * c - im * s, im * c + re * s


def fft4(x, sign):
    (ar, ai), (br, bi), (cr, ci), (dr, di) = x
    er, ei, fr, fi = ar + cr, ai + ci, ar - cr, ai - ci
    gr, gi, hr, hi = br + dr, bi + di, br - dr, bi - di
    if sign < 0:
        jr, ji = hi, -hr
    else:
        jr, ji = -hi, hr
    return [(er + gr, ei + gi), (fr + jr, fi + ji), (er - gr, ei - gi), (fr - jr, fi - ji)]


def fft8(x, sign):
    even = fft4(x[0::2], sign)
    odd = fft4(x[1::2], sign)
    o1r, o1i = odd[1]
    o2r, o2i = odd[2]
    o3r, o3i = odd[3]
    if sign < 0:
        odd[1] = ((o1r + o1i) * HALF_ROOT, (o1i - o1r) * HALF_ROOT)
        odd[2] = (o2i, -o2r)
        odd[3] = ((o3i - o3r) * HALF_ROOT, (-o3i - o3r) * HALF_ROOT)
    else:
        odd[1] = ((o1r - o1i) * HALF_ROOT, (o1i + o1r) * HALF_ROOT)
        odd[2] = (-o2i, o2r)
        odd[3] = ((-o3r - o3i) * HALF_ROOT, (o3r - o3i) * HALF_ROOT)
    low = [(e[0] + o[0], e[1] + o[1]) for e, o in zip(even, odd)]
    high = [(e[0] - o[0], e[1] - o[1]) for e, o in zip(even, odd)]
    return low + high


def store_split(high_ref, low_ref, index, value):
    high = value.astype(BF16)
    high_ref[index] = high
    low_ref[index] = (value - high.astype(F32)).astype(BF16)


def forward_blocks(source, half, mid, high_ref, low_ref, twiddle):
    for k2 in range(8):
        x = [source[k2 + 8 * k1, half].astype(F32) for k1 in range(4)]
        x0, x1, x2, x3 = x

        def real_times(value, angle):
            return value * float(np.cos(angle)), value * float(np.sin(angle))

        t1 = real_times(x1, -2 * np.pi / 16)
        t2 = real_times(x2, -2 * np.pi * 2 / 16)
        t3 = real_times(x3, -2 * np.pi * 3 / 16)
        er, ei, fr, fi = x0 + t2[0], t2[1], x0 - t2[0], -t2[1]
        gr, gi, hr, hi = t1[0] + t3[0], t1[1] + t3[1], t1[0] - t3[0], t1[1] - t3[1]
        results = [(er + gr, ei + gi), (fr + hi, fi - hr), (er - gr, ei - gi), (fr - hi, fi + hr)]
        for f1 in range(4):
            re, im = times(results[f1], -2 * np.pi * k2 * (0.25 + f1) / 32)
            mid[0, f1, k2] = re
            mid[1, f1, k2] = im
    for f1 in range(4):
        spectrum = fft8([(mid[0, f1, k2], mid[1, f1, k2]) for k2 in range(8)], -1)
        for f2 in range(8):
            f = f1 + 4 * f2
            c = twiddle[0, f : f + 1, :]
            s = twiddle[1, f : f + 1, :]
            re, im = spectrum[f2]
            rows = pl.ds(f * ROWS, ROWS)
            store_split(high_ref, low_ref, (rows, pl.ds(0, LANES)), re * c + im * s)
            store_split(high_ref, low_ref, (rows, pl.ds(LANES, LANES)), im * c - re * s)


def inverse_blocks(source, mid, out, half, twiddle):
    for f1 in range(4):
        values = []
        for f2 in range(8):
            f = f1 + 4 * f2
            c = twiddle[0, f : f + 1, :]
            s = twiddle[1, f : f + 1, :]
            re = source[pl.ds(f * ROWS, ROWS), pl.ds(0, LANES)]
            im = source[pl.ds(f * ROWS, ROWS), pl.ds(LANES, LANES)]
            values.append((re * c - im * s, im * c + re * s))
        spectrum = fft8(values, 1)
        for k2 in range(8):
            re, im = times(spectrum[k2], 2 * np.pi * k2 * (0.25 + f1) / 32)
            mid[0, f1, k2] = re
            mid[1, f1, k2] = im
    for k2 in range(8):
        u = fft4([(mid[0, f1, k2], mid[1, f1, k2]) for f1 in range(4)], 1)
        for k1 in range(4):
            angle = 2 * np.pi * k1 / 16
            re, im = u[k1]
            y = re if k1 == 0 else re * float(np.cos(angle)) - im * float(np.sin(angle))
            out[k2 + 8 * k1, half] = y.astype(BF16)


def dot(a, b):
    return jnp.dot(a, b, preferred_element_type=F32)


CHUNK = 128
SPECTRUM_ROWS = BLOCKS * ROWS


def filter_spectrum(high_ref, low_ref, dft, out, half):
    def step(i, carry):
        rows = pl.ds(pl.multiple_of(i * CHUNK, CHUNK), CHUNK)
        high, low = high_ref[rows, :], low_ref[rows, :]
        out[half, rows, :] = dot(high, dft[0]) + dot(low, dft[0]) + dot(high, dft[1])
        return carry

    lax.fori_loop(0, SPECTRUM_ROWS // CHUNK, step, 0)


def multiply_spectra(high_ref, low_ref, dft, filters, half, out):
    def step(i, carry):
        rows = pl.ds(pl.multiple_of(i * CHUNK, CHUNK), CHUNK)
        high, low = high_ref[rows, :], low_ref[rows, :]
        g = dot(high, dft[0]) + dot(low, dft[0]) + dot(high, dft[1])
        h = filters[half, rows, :]
        gr, gi, hr, hi = g[:, :LANES], g[:, LANES:], h[:, :LANES], h[:, LANES:]
        product = jnp.concatenate([gr * hr - gi * hi, gr * hi + gi * hr], axis=1)
        high = product.astype(BF16)
        low = (product - high.astype(F32)).astype(BF16)
        out[rows, :] = dot(high, dft[2]) + dot(low, dft[2]) + dot(high, dft[3])
        return carry

    lax.fori_loop(0, SPECTRUM_ROWS // CHUNK, step, 0)


def kernel(
    q_hbm, k_hbm, v_hbm, fw_ref, h_hbm, skip_ref, w_hbm, tw_hbm, dft_hbm,
    out_ref,
    q_in, k_in, v_in, h_in, w_in, twiddle, dft,
    tails, halo, extended, query, gated,
    h_send, g_send, y_send, h_all, g_all, y_all,
    mid, high_ref, low_ref, h_spec, v_spec, mixed, total,
    local_sem, halo_sem, h_sem, g_sem, y_sem, m_sem,
):
    n = lax.axis_size("seq")
    me = lax.axis_index("seq")
    mine = lax.axis_index("ch")
    across = lax.rem(mine + 2, 4)
    beside = mine + 1 - 2 * lax.rem(mine, 2)
    diagonal = lax.rem(beside + 2, 4)

    local = [
        pltpu.make_async_copy(source, target, local_sem.at[i])
        for i, (source, target) in enumerate(
            [(q_hbm, q_in), (k_hbm, k_in), (v_hbm, v_in), (h_hbm, h_in), (tw_hbm, twiddle), (dft_hbm, dft), (w_hbm, w_in)]
        )
    ]
    for copy in local:
        copy.start()

    barrier = pltpu.get_barrier_semaphore()

    def greet(s, carry):
        pl.semaphore_signal(barrier, inc=1, device_id={"seq": lax.rem(me + s, n)}, device_id_type=MESH)
        return carry

    lax.fori_loop(1, n, greet, 0)
    for peer in (across, beside):
        pl.semaphore_signal(barrier, inc=1, device_id={"ch": peer}, device_id_type=MESH)

    for i in range(3):
        local[i].wait()
    for i, x in enumerate((q_in, k_in, v_in)):
        tails[i] = x[112:128, :].astype(F32)[8:16, :]
    local[3].wait()

    def turn(source, target):
        def step(i, carry):
            cols = pl.ds(pl.multiple_of(i * 128, 128), 128)
            block = source[:, cols].T.astype(BF16).reshape(8, ROWS, LANES)
            target[i // 4, pl.ds(lax.rem(i, 4) * 8, 8)] = block
            return carry

        lax.fori_loop(0, 8, step, 0)

    turn(h_in, h_send)

    pl.semaphore_wait(barrier, n - 1 + 2)

    halo_copy = pltpu.make_async_remote_copy(
        src_ref=tails, dst_ref=halo, send_sem=halo_sem.at[0], recv_sem=halo_sem.at[1],
        device_id={"seq": lax.rem(me + 1, n)}, device_id_type=MESH,
    )
    halo_copy.start()

    def scatter(source, target, sems):
        def step(s, carry):
            peer = lax.rem(me + s, n)
            pltpu.make_async_remote_copy(
                src_ref=source.at[:, peer], dst_ref=target.at[me], send_sem=sems.at[0], recv_sem=sems.at[1],
                device_id={"seq": peer}, device_id_type=MESH,
            ).start()
            return carry

        lax.fori_loop(1, n, step, 0)
        target[me] = source[:, me]

    def all_of(ref, sems):
        part = ref.at[pl.ds(0, BLOCKS - 1)]
        return pltpu.make_async_remote_copy(
            src_ref=part, dst_ref=part, send_sem=sems.at[0], recv_sem=sems.at[1],
            device_id={"seq": lax.rem(me + 1, n)}, device_id_type=MESH,
        )

    scatter(h_send, h_all, h_sem)

    halo_copy.wait()
    keep = jnp.where(me == 0, 0.0, 1.0).astype(F32)
    for i, x in enumerate((q_in, k_in, v_in)):
        extended[i, 0:8, :] = halo[i] * keep

        def widen(r, carry):
            rows = pl.multiple_of(r * 16, 16)
            extended[i, pl.ds(rows + 8, 16), :] = x[pl.ds(rows, 16), :].astype(F32)
            return carry

        lax.fori_loop(0, 8, widen, 0)

    def feature(i, cols):
        result = fw_ref[i, 0:1, cols] * extended[i, 8:136, cols]
        result += fw_ref[i, 1:2, cols] * extended[i, 7:135, cols]
        return result + fw_ref[i, 2:3, cols] * extended[i, 6:134, cols]

    def gate(i, carry):
        cols = pl.ds(pl.multiple_of(i * 128, 128), 128)
        value = feature(1, cols) * feature(2, cols)
        gated[:, cols] = value
        g_send[i // 4, pl.ds(lax.rem(i, 4) * 8, 8)] = value.T.astype(BF16).reshape(8, ROWS, LANES)
        return carry

    lax.fori_loop(0, 8, gate, 0)
    scatter(g_send, g_all, g_sem)

    def queries(i, carry):
        cols = pl.ds(pl.multiple_of(i * 128, 128), 128)
        query[:, cols] = feature(0, cols)
        gated[:, cols] = gated[:, cols] * skip_ref[0:1, cols]
        return carry

    lax.fori_loop(0, 8, queries, 0)

    local[4].wait()
    local[5].wait()
    all_of(h_all, h_sem).wait_recv()

    def filters(half, carry):
        forward_blocks(h_all, half, mid, high_ref, low_ref, twiddle)
        filter_spectrum(high_ref, low_ref, dft, h_spec, half)
        return carry

    lax.fori_loop(0, 2, filters, 0)
    all_of(g_all, g_sem).wait_recv()

    def convolve(half, carry):
        forward_blocks(g_all, half, mid, high_ref, low_ref, twiddle)
        multiply_spectra(high_ref, low_ref, dft, h_spec, half, v_spec)
        inverse_blocks(v_spec, mid, y_send, half, twiddle)

        def step(s, inner):
            peer = lax.rem(me + s, n)
            pltpu.make_async_remote_copy(
                src_ref=y_send.at[peer, half], dst_ref=y_all.at[half, me],
                send_sem=y_sem.at[0, half], recv_sem=y_sem.at[1, half],
                device_id={"seq": peer}, device_id_type=MESH,
            ).start()
            return inner

        lax.fori_loop(1, n, step, 0)
        y_all[half, me] = y_send[me, half]
        return carry

    lax.fori_loop(0, 2, convolve, 0)

    def y_done(half):
        part = y_all.at[half, pl.ds(0, BLOCKS - 1)]
        return pltpu.make_async_remote_copy(
            src_ref=part, dst_ref=part, send_sem=y_sem.at[0, half], recv_sem=y_sem.at[1, half],
            device_id={"seq": lax.rem(me + 1, n)}, device_id_type=MESH,
        )

    def share(slot, half, peer, index):
        return pltpu.make_async_remote_copy(
            src_ref=mixed.at[slot, half], dst_ref=mixed.at[slot, half],
            send_sem=m_sem.at[0, index, half], recv_sem=m_sem.at[1, index, half],
            device_id={"ch": peer}, device_id_type=MESH,
        )

    def project(slot, half, first=False):
        rows = pl.ds(pl.multiple_of(slot * 1024 + half * 512, 512), 512)

        def step(j, carry):
            cols = pl.ds(pl.multiple_of(j * 256, 256), 256)
            value = dot(mixed[slot, half], w_in[rows, cols])
            total[:, cols] = value if first else total[:, cols] + value
            return carry

        lax.fori_loop(0, 4, step, 0)

    for half in range(2):
        y_done(half).wait_recv()

        def mix(i, carry):
            cols = pl.ds(pl.multiple_of(half * 512 + i * 128, 128), 128)
            y = y_all[half, pl.ds(i * 8, 8)].astype(F32).reshape(128, LANES).T
            mixed[mine, half, :, pl.ds(pl.multiple_of(i * 128, 128), 128)] = (
                query[:, cols] * (y + gated[:, cols])
            ).astype(BF16)
            return carry

        lax.fori_loop(0, 4, mix, 0)
        share(mine, half, across, 0).start()
        share(mine, half, beside, 1).start()
    local[6].wait()
    for half in range(2):
        project(mine, half, first=half == 0)
        share(across, half, across, 0).wait_recv()
        share(across, half, beside, 2).start()
        project(across, half)
    for half in range(2):
        share(beside, half, beside, 1).wait_recv()
        project(beside, half)
    for half in range(2):
        share(diagonal, half, beside, 2).wait_recv()
        project(diagonal, half)

    def finish(j, carry):
        cols = pl.ds(pl.multiple_of(j * 256, 256), 256)
        out_ref[:, cols] = total[:, cols].astype(BF16)
        return carry

    lax.fori_loop(0, 4, finish, 0)

    all_of(h_all, h_sem).wait_send()
    all_of(g_all, g_sem).wait_send()
    for half in range(2):
        y_done(half).wait_send()
        share(mine, half, across, 0).wait_send()
        share(mine, half, beside, 1).wait_send()
        share(across, half, beside, 2).wait_send()


def shards(query_proj, key_proj, value_proj, feat_weight, long_filter, skip_gain, out_weight):
    twiddle, dft = tables()
    anywhere = pl.BlockSpec(memory_space=pl.ANY)
    vmem = pl.BlockSpec(memory_space=pltpu.VMEM)
    tokens, channels = query_proj.shape
    spectrum = (SPECTRUM_ROWS, 2 * LANES)
    exchanged = (BLOCKS, 2, ROWS, LANES)
    turned = (2, BLOCKS, ROWS, LANES)
    return pl.pallas_call(
        kernel,
        out_shape=jax.ShapeDtypeStruct((tokens, channels), BF16),
        in_specs=[anywhere, anywhere, anywhere, vmem, anywhere, vmem, anywhere, anywhere, anywhere],
        out_specs=vmem,
        scratch_shapes=[
            pltpu.VMEM((tokens, channels), BF16),
            pltpu.VMEM((tokens, channels), BF16),
            pltpu.VMEM((tokens, channels), BF16),
            pltpu.VMEM((tokens, channels), F32),
            pltpu.VMEM(out_weight.shape, BF16),
            pltpu.VMEM(twiddle.shape, F32),
            pltpu.VMEM(dft.shape, BF16),
            pltpu.VMEM((3, 8, channels), F32),
            pltpu.VMEM((3, 8, channels), F32),
            pltpu.VMEM((3, tokens + 8, channels), F32),
            pltpu.VMEM((tokens, channels), F32),
            pltpu.VMEM((tokens, channels), F32),
            pltpu.VMEM(turned, BF16),
            pltpu.VMEM(turned, BF16),
            pltpu.VMEM(exchanged, BF16),
            pltpu.VMEM(exchanged, BF16),
            pltpu.VMEM(exchanged, BF16),
            pltpu.VMEM(turned, BF16),
            pltpu.VMEM((2, 4, 8, ROWS, LANES), F32),
            pltpu.VMEM(spectrum, BF16),
            pltpu.VMEM(spectrum, BF16),
            pltpu.VMEM((2,) + spectrum, F32),
            pltpu.VMEM(spectrum, F32),
            pltpu.VMEM((4, 2, tokens, channels // 2), BF16),
            pltpu.VMEM((tokens, channels), F32),
            pltpu.SemaphoreType.DMA((7,)),
            pltpu.SemaphoreType.DMA((2,)),
            pltpu.SemaphoreType.DMA((2,)),
            pltpu.SemaphoreType.DMA((2,)),
            pltpu.SemaphoreType.DMA((2, 2)),
            pltpu.SemaphoreType.DMA((2, 3, 2)),
        ],
        compiler_params=pltpu.CompilerParams(
            collective_id=0, has_side_effects=True, vmem_limit_bytes=56 * 1024 * 1024
        ),
        name="mixer",
    )(
        query_proj, key_proj, value_proj, feat_weight, long_filter, skip_gain[None, :], out_weight, twiddle, dft,
    )


def solution(mesh):
    placed = (
        P("seq", "ch"),
        P("seq", "ch"),
        P("seq", "ch"),
        P(None, None, "ch"),
        P("seq", "ch"),
        P("ch"),
        P(None, "ch"),
    )
    return jax.shard_map(shards, mesh=mesh, in_specs=placed, out_specs=P("seq", "ch"), check_vma=False)
```

```python
import functools

import jax
import jax.numpy as jnp
import numpy as np
from jax import lax
from jax.experimental import pallas as pl
from jax.experimental.pallas import tpu as pltpu
from jax.sharding import PartitionSpec as P

F32 = jnp.float32
BF16 = jnp.bfloat16
MESH = pl.DeviceIdType.MESH
BLOCKS = 32
LANES = 128
ROWS = 16
FAR_FIRST = sorted(
    ((dx, dy, dz) for dx in range(4) for dy in range(2) for dz in range(4) if dx + dy + dz),
    key=lambda d: -(min(d[0], 4 - d[0]) + d[1] + min(d[2], 4 - d[2])),
)
HALF_ROOT = float(np.sqrt(0.5))


def tables():
    lane = np.arange(LANES)
    theta = 2 * np.pi * (np.arange(BLOCKS)[:, None] + 0.25) * lane[None, :] / (BLOCKS * LANES)
    twiddle = np.stack([np.cos(theta), np.sin(theta)]).astype(np.float32)
    phase = 2 * np.pi * (lane[:, None] * lane[None, :] % LANES) / LANES
    c, s = np.cos(phase), np.sin(phase)
    forward = np.block([[c, -s], [s, c]])
    inverse = np.block([[c, s], [-s, c]]) / (BLOCKS * LANES)
    parts = []
    for matrix in (forward, inverse):
        high = matrix.astype(BF16)
        parts += [high, (matrix - high.astype(np.float64)).astype(BF16)]
    return jnp.asarray(twiddle), jnp.asarray(np.stack(parts))


def times(value, angle):
    re, im = value
    c, s = float(np.cos(angle)), float(np.sin(angle))
    if abs(angle) < 1e-12:
        return re, im
    return re * c - im * s, im * c + re * s


def fft4(x, sign):
    (ar, ai), (br, bi), (cr, ci), (dr, di) = x
    er, ei, fr, fi = ar + cr, ai + ci, ar - cr, ai - ci
    gr, gi, hr, hi = br + dr, bi + di, br - dr, bi - di
    if sign < 0:
        jr, ji = hi, -hr
    else:
        jr, ji = -hi, hr
    return [(er + gr, ei + gi), (fr + jr, fi + ji), (er - gr, ei - gi), (fr - jr, fi - ji)]


def fft8(x, sign):
    even = fft4(x[0::2], sign)
    odd = fft4(x[1::2], sign)
    o1r, o1i = odd[1]
    o2r, o2i = odd[2]
    o3r, o3i = odd[3]
    if sign < 0:
        odd[1] = ((o1r + o1i) * HALF_ROOT, (o1i - o1r) * HALF_ROOT)
        odd[2] = (o2i, -o2r)
        odd[3] = ((o3i - o3r) * HALF_ROOT, (-o3i - o3r) * HALF_ROOT)
    else:
        odd[1] = ((o1r - o1i) * HALF_ROOT, (o1i + o1r) * HALF_ROOT)
        odd[2] = (-o2i, o2r)
        odd[3] = ((-o3r - o3i) * HALF_ROOT, (o3r - o3i) * HALF_ROOT)
    low = [(e[0] + o[0], e[1] + o[1]) for e, o in zip(even, odd)]
    high = [(e[0] - o[0], e[1] - o[1]) for e, o in zip(even, odd)]
    return low + high


def store_split(high_ref, low_ref, index, value):
    high = value.astype(BF16)
    high_ref[index] = high
    low_ref[index] = (value - high.astype(F32)).astype(BF16)


def forward_blocks(source, half, mid, high_ref, low_ref, twiddle):
    for k2 in range(8):
        x = [source[half, k2 + 8 * k1].astype(F32) for k1 in range(4)]
        x0, x1, x2, x3 = x

        def real_times(value, angle):
            return value * float(np.cos(angle)), value * float(np.sin(angle))

        t1 = real_times(x1, -2 * np.pi / 16)
        t2 = real_times(x2, -2 * np.pi * 2 / 16)
        t3 = real_times(x3, -2 * np.pi * 3 / 16)
        er, ei, fr, fi = x0 + t2[0], t2[1], x0 - t2[0], -t2[1]
        gr, gi, hr, hi = t1[0] + t3[0], t1[1] + t3[1], t1[0] - t3[0], t1[1] - t3[1]
        results = [(er + gr, ei + gi), (fr + hi, fi - hr), (er - gr, ei - gi), (fr - hi, fi + hr)]
        for f1 in range(4):
            re, im = times(results[f1], -2 * np.pi * k2 * (0.25 + f1) / 32)
            mid[0, f1, k2] = re
            mid[1, f1, k2] = im
    for f1 in range(4):
        spectrum = fft8([(mid[0, f1, k2], mid[1, f1, k2]) for k2 in range(8)], -1)
        for f2 in range(8):
            f = f1 + 4 * f2
            c = twiddle[0, f : f + 1, :]
            s = twiddle[1, f : f + 1, :]
            re, im = spectrum[f2]
            rows = pl.ds(f * ROWS, ROWS)
            store_split(high_ref, low_ref, (rows, pl.ds(0, LANES)), re * c + im * s)
            store_split(high_ref, low_ref, (rows, pl.ds(LANES, LANES)), im * c - re * s)


def inverse_blocks(source, mid, out, half, twiddle):
    for f1 in range(4):
        values = []
        for f2 in range(8):
            f = f1 + 4 * f2
            c = twiddle[0, f : f + 1, :]
            s = twiddle[1, f : f + 1, :]
            re = source[pl.ds(f * ROWS, ROWS), pl.ds(0, LANES)]
            im = source[pl.ds(f * ROWS, ROWS), pl.ds(LANES, LANES)]
            values.append((re * c - im * s, im * c + re * s))
        spectrum = fft8(values, 1)
        for k2 in range(8):
            re, im = times(spectrum[k2], 2 * np.pi * k2 * (0.25 + f1) / 32)
            mid[0, f1, k2] = re
            mid[1, f1, k2] = im
    for k2 in range(8):
        u = fft4([(mid[0, f1, k2], mid[1, f1, k2]) for f1 in range(4)], 1)
        for k1 in range(4):
            angle = 2 * np.pi * k1 / 16
            re, im = u[k1]
            y = re if k1 == 0 else re * float(np.cos(angle)) - im * float(np.sin(angle))
            out[half, k2 + 8 * k1] = y.astype(BF16)


def dot(a, b):
    return jnp.dot(a, b, preferred_element_type=F32)


CHUNK = 128
SPECTRUM_ROWS = BLOCKS * ROWS


def filter_spectrum(high_ref, low_ref, dft, out, half):
    def step(i, carry):
        rows = pl.ds(pl.multiple_of(i * CHUNK, CHUNK), CHUNK)
        high, low = high_ref[rows, :], low_ref[rows, :]
        out[half, rows, :] = dot(high, dft[0]) + dot(low, dft[0]) + dot(high, dft[1])
        return carry

    lax.fori_loop(0, SPECTRUM_ROWS // CHUNK, step, 0)


def multiply_spectra(high_ref, low_ref, dft, filters, half, out):
    def step(i, carry):
        rows = pl.ds(pl.multiple_of(i * CHUNK, CHUNK), CHUNK)
        high, low = high_ref[rows, :], low_ref[rows, :]
        g = dot(high, dft[0]) + dot(low, dft[0]) + dot(high, dft[1])
        h = filters[half, rows, :]
        gr, gi, hr, hi = g[:, :LANES], g[:, LANES:], h[:, :LANES], h[:, LANES:]
        product = jnp.concatenate([gr * hr - gi * hi, gr * hi + gi * hr], axis=1)
        high = product.astype(BF16)
        low = (product - high.astype(F32)).astype(BF16)
        out[rows, :] = dot(high, dft[2]) + dot(low, dft[2]) + dot(high, dft[3])
        return carry

    lax.fori_loop(0, SPECTRUM_ROWS // CHUNK, step, 0)


def kernel(
    q_hbm, k_hbm, v_hbm, fw_ref, h_hbm, skip_ref, w_hbm, tw_hbm, dft_hbm,
    out_ref,
    q_in, k_in, v_in, h_in, w_in, twiddle, dft,
    tails, halo, extended, query, gated,
    h_send, g_send, y_send, h_all, g_all, y_all,
    mid, high_ref, low_ref, h_spec, v_spec, mixed, total,
    local_sem, halo_sem, h_sem, g_sem, y_sem, m_sem,
):
    n = lax.axis_size("seq")
    me = lax.axis_index("seq")
    mine = lax.axis_index("ch")
    across = lax.rem(mine + 2, 4)
    beside = mine + 1 - 2 * lax.rem(mine, 2)
    diagonal = lax.rem(beside + 2, 4)

    local = [
        pltpu.make_async_copy(source, target, local_sem.at[i])
        for i, (source, target) in enumerate(
            [(q_hbm, q_in), (k_hbm, k_in), (v_hbm, v_in), (h_hbm, h_in), (tw_hbm, twiddle), (dft_hbm, dft), (w_hbm, w_in)]
        )
    ]
    for copy in local:
        copy.start()

    barrier = pltpu.get_barrier_semaphore()

    def greet(s, carry):
        pl.semaphore_signal(barrier, inc=1, device_id={"seq": lax.rem(me + s, n)}, device_id_type=MESH)
        return carry

    lax.fori_loop(1, n, greet, 0)
    for peer in (across, beside):
        pl.semaphore_signal(barrier, inc=1, device_id={"ch": peer}, device_id_type=MESH)

    for i in range(3):
        local[i].wait()
    for i, x in enumerate((q_in, k_in, v_in)):
        tails[i] = x[112:128, :].astype(F32)[8:16, :]
    local[3].wait()

    def turn(source, target):
        def step(i, carry):
            cols = pl.ds(pl.multiple_of(i * 128, 128), 128)
            block = source[:, cols].T.astype(BF16).reshape(8, ROWS, LANES)
            target[i // 4, pl.ds(lax.rem(i, 4) * 8, 8)] = block
            return carry

        lax.fori_loop(0, 8, step, 0)

    turn(h_in, h_send)

    pl.semaphore_wait(barrier, n - 1 + 2)

    halo_copy = pltpu.make_async_remote_copy(
        src_ref=tails, dst_ref=halo, send_sem=halo_sem.at[0], recv_sem=halo_sem.at[1],
        device_id={"seq": lax.rem(me + 1, n)}, device_id_type=MESH,
    )
    halo_copy.start()

    xs = [lax.rem(me // 8 + d, 4) * 8 for d in range(4)]
    ys = [lax.rem(me // 4 + d, 2) * 4 for d in range(2)]
    zs = [lax.rem(me + d, 4) for d in range(4)]

    def scatter(source, target, half, sems):
        for dx, dy, dz in FAR_FIRST:
            peer = xs[dx] + ys[dy] + zs[dz]
            pltpu.make_async_remote_copy(
                src_ref=source.at[half, peer], dst_ref=target.at[half, me],
                send_sem=sems.at[0, half], recv_sem=sems.at[1, half],
                device_id={"seq": peer}, device_id_type=MESH,
            ).start()
        target[half, me] = source[half, me]

    def all_of(ref, half, sems):
        part = ref.at[half, pl.ds(0, BLOCKS - 1)]
        return pltpu.make_async_remote_copy(
            src_ref=part, dst_ref=part, send_sem=sems.at[0, half], recv_sem=sems.at[1, half],
            device_id={"seq": lax.rem(me + 1, n)}, device_id_type=MESH,
        )

    scatter(h_send, h_all, 0, h_sem)
    scatter(h_send, h_all, 1, h_sem)

    halo_copy.wait()
    keep = jnp.where(me == 0, 0.0, 1.0).astype(F32)
    for i, x in enumerate((q_in, k_in, v_in)):
        extended[i, 0:8, :] = halo[i] * keep

        def widen(r, carry):
            rows = pl.multiple_of(r * 16, 16)
            extended[i, pl.ds(rows + 8, 16), :] = x[pl.ds(rows, 16), :].astype(F32)
            return carry

        lax.fori_loop(0, 8, widen, 0)

    def feature(i, cols):
        result = fw_ref[i, 0:1, cols] * extended[i, 8:136, cols]
        result += fw_ref[i, 1:2, cols] * extended[i, 7:135, cols]
        return result + fw_ref[i, 2:3, cols] * extended[i, 6:134, cols]

    def gate(i, carry):
        cols = pl.ds(pl.multiple_of(i * 128, 128), 128)
        value = feature(1, cols) * feature(2, cols)
        gated[:, cols] = value
        g_send[i // 4, pl.ds(lax.rem(i, 4) * 8, 8)] = value.T.astype(BF16).reshape(8, ROWS, LANES)
        return carry

    for half in range(2):
        lax.fori_loop(4 * half, 4 * half + 4, gate, 0)
        scatter(g_send, g_all, half, g_sem)

    def queries(i, carry):
        cols = pl.ds(pl.multiple_of(i * 128, 128), 128)
        query[:, cols] = feature(0, cols)
        gated[:, cols] = gated[:, cols] * skip_ref[0:1, cols]
        return carry

    lax.fori_loop(0, 8, queries, 0)

    local[4].wait()
    local[5].wait()

    def filters(half, carry):
        all_of(h_all, half, h_sem).wait_recv()
        forward_blocks(h_all, half, mid, high_ref, low_ref, twiddle)
        filter_spectrum(high_ref, low_ref, dft, h_spec, half)
        return carry

    lax.fori_loop(0, 2, filters, 0)

    def convolve(half, carry):
        all_of(g_all, half, g_sem).wait_recv()
        forward_blocks(g_all, half, mid, high_ref, low_ref, twiddle)
        multiply_spectra(high_ref, low_ref, dft, h_spec, half, v_spec)
        inverse_blocks(v_spec, mid, y_send, half, twiddle)
        scatter(y_send, y_all, half, y_sem)
        return carry

    lax.fori_loop(0, 2, convolve, 0)

    def share(slot, half, peer, index):
        return pltpu.make_async_remote_copy(
            src_ref=mixed.at[slot, half], dst_ref=mixed.at[slot, half],
            send_sem=m_sem.at[0, index, half], recv_sem=m_sem.at[1, index, half],
            device_id={"ch": peer}, device_id_type=MESH,
        )

    def project(slot, half, first=False):
        rows = pl.ds(pl.multiple_of(slot * 1024 + half * 512, 512), 512)

        def step(j, carry):
            cols = pl.ds(pl.multiple_of(j * 256, 256), 256)
            value = dot(mixed[slot, half], w_in[rows, cols])
            total[:, cols] = value if first else total[:, cols] + value
            return carry

        lax.fori_loop(0, 4, step, 0)

    for half in range(2):
        all_of(y_all, half, y_sem).wait_recv()

        def mix(i, carry):
            cols = pl.ds(pl.multiple_of(half * 512 + i * 128, 128), 128)
            y = y_all[half, pl.ds(i * 8, 8)].astype(F32).reshape(128, LANES).T
            mixed[mine, half, :, pl.ds(pl.multiple_of(i * 128, 128), 128)] = (
                query[:, cols] * (y + gated[:, cols])
            ).astype(BF16)
            return carry

        lax.fori_loop(0, 4, mix, 0)
        share(mine, half, across, 0).start()
        share(mine, half, beside, 1).start()
    local[6].wait()
    for half in range(2):
        project(mine, half, first=half == 0)
        share(across, half, across, 0).wait_recv()
        share(across, half, beside, 2).start()
        project(across, half)
    for half in range(2):
        share(beside, half, beside, 1).wait_recv()
        project(beside, half)
    for half in range(2):
        share(diagonal, half, beside, 2).wait_recv()
        project(diagonal, half)

    def finish(j, carry):
        cols = pl.ds(pl.multiple_of(j * 256, 256), 256)
        out_ref[:, cols] = total[:, cols].astype(BF16)
        return carry

    lax.fori_loop(0, 4, finish, 0)

    for half in range(2):
        all_of(h_all, half, h_sem).wait_send()
        all_of(g_all, half, g_sem).wait_send()
        all_of(y_all, half, y_sem).wait_send()
        share(mine, half, across, 0).wait_send()
        share(mine, half, beside, 1).wait_send()
        share(across, half, beside, 2).wait_send()


def shards(query_proj, key_proj, value_proj, feat_weight, long_filter, skip_gain, out_weight):
    twiddle, dft = tables()
    anywhere = pl.BlockSpec(memory_space=pl.ANY)
    vmem = pl.BlockSpec(memory_space=pltpu.VMEM)
    tokens, channels = query_proj.shape
    spectrum = (SPECTRUM_ROWS, 2 * LANES)
    turned = (2, BLOCKS, ROWS, LANES)
    return pl.pallas_call(
        kernel,
        out_shape=jax.ShapeDtypeStruct((tokens, channels), BF16),
        in_specs=[anywhere, anywhere, anywhere, vmem, anywhere, vmem, anywhere, anywhere, anywhere],
        out_specs=vmem,
        scratch_shapes=[
            pltpu.VMEM((tokens, channels), BF16),
            pltpu.VMEM((tokens, channels), BF16),
            pltpu.VMEM((tokens, channels), BF16),
            pltpu.VMEM((tokens, channels), F32),
            pltpu.VMEM(out_weight.shape, BF16),
            pltpu.VMEM(twiddle.shape, F32),
            pltpu.VMEM(dft.shape, BF16),
            pltpu.VMEM((3, 8, channels), F32),
            pltpu.VMEM((3, 8, channels), F32),
            pltpu.VMEM((3, tokens + 8, channels), F32),
            pltpu.VMEM((tokens, channels), F32),
            pltpu.VMEM((tokens, channels), F32),
            pltpu.VMEM(turned, BF16),
            pltpu.VMEM(turned, BF16),
            pltpu.VMEM(turned, BF16),
            pltpu.VMEM(turned, BF16),
            pltpu.VMEM(turned, BF16),
            pltpu.VMEM(turned, BF16),
            pltpu.VMEM((2, 4, 8, ROWS, LANES), F32),
            pltpu.VMEM(spectrum, BF16),
            pltpu.VMEM(spectrum, BF16),
            pltpu.VMEM((2,) + spectrum, F32),
            pltpu.VMEM(spectrum, F32),
            pltpu.VMEM((4, 2, tokens, channels // 2), BF16),
            pltpu.VMEM((tokens, channels), F32),
            pltpu.SemaphoreType.DMA((7,)),
            pltpu.SemaphoreType.DMA((2,)),
            pltpu.SemaphoreType.DMA((2, 2)),
            pltpu.SemaphoreType.DMA((2, 2)),
            pltpu.SemaphoreType.DMA((2, 2)),
            pltpu.SemaphoreType.DMA((2, 3, 2)),
        ],
        compiler_params=pltpu.CompilerParams(
            collective_id=0, has_side_effects=True, vmem_limit_bytes=56 * 1024 * 1024
        ),
        name="mixer",
    )(
        query_proj, key_proj, value_proj, feat_weight, long_filter, skip_gain[None, :], out_weight, twiddle, dft,
    )


def solution(mesh):
    placed = (
        P("seq", "ch"),
        P("seq", "ch"),
        P("seq", "ch"),
        P(None, None, "ch"),
        P("seq", "ch"),
        P("ch"),
        P(None, "ch"),
    )
    return jax.shard_map(shards, mesh=mesh, in_specs=placed, out_specs=P("seq", "ch"), check_vma=False)
```

```python
import functools

import jax
import jax.numpy as jnp
import numpy as np
from jax import lax
from jax.experimental import pallas as pl
from jax.experimental.pallas import tpu as pltpu
from jax.sharding import PartitionSpec as P

F32 = jnp.float32
BF16 = jnp.bfloat16
MESH = pl.DeviceIdType.MESH
BLOCKS = 32
LANES = 128
PARTS = 2
ROWS = 32 // PARTS
WIDTH = BLOCKS * ROWS
TILES = 128 // ROWS
FAR_FIRST = sorted(
    ((dx, dy, dz) for dx in range(4) for dy in range(2) for dz in range(4) if dx + dy + dz),
    key=lambda d: -(min(d[0], 4 - d[0]) + d[1] + min(d[2], 4 - d[2])),
)
HALF_ROOT = float(np.sqrt(0.5))


def tables():
    lane = np.arange(LANES)
    theta = 2 * np.pi * (np.arange(BLOCKS)[:, None] + 0.25) * lane[None, :] / (BLOCKS * LANES)
    twiddle = np.stack([np.cos(theta), np.sin(theta)]).astype(np.float32)
    phase = 2 * np.pi * (lane[:, None] * lane[None, :] % LANES) / LANES
    c, s = np.cos(phase), np.sin(phase)
    forward = np.block([[c, -s], [s, c]])
    inverse = np.block([[c, s], [-s, c]]) / (BLOCKS * LANES)
    parts = []
    for matrix in (forward, inverse):
        high = matrix.astype(BF16)
        parts += [high, (matrix - high.astype(np.float64)).astype(BF16)]
    return jnp.asarray(twiddle), jnp.asarray(np.stack(parts))


def times(value, angle):
    re, im = value
    c, s = float(np.cos(angle)), float(np.sin(angle))
    if abs(angle) < 1e-12:
        return re, im
    return re * c - im * s, im * c + re * s


def fft4(x, sign):
    (ar, ai), (br, bi), (cr, ci), (dr, di) = x
    er, ei, fr, fi = ar + cr, ai + ci, ar - cr, ai - ci
    gr, gi, hr, hi = br + dr, bi + di, br - dr, bi - di
    if sign < 0:
        jr, ji = hi, -hr
    else:
        jr, ji = -hi, hr
    return [(er + gr, ei + gi), (fr + jr, fi + ji), (er - gr, ei - gi), (fr - jr, fi - ji)]


def fft8(x, sign):
    even = fft4(x[0::2], sign)
    odd = fft4(x[1::2], sign)
    o1r, o1i = odd[1]
    o2r, o2i = odd[2]
    o3r, o3i = odd[3]
    if sign < 0:
        odd[1] = ((o1r + o1i) * HALF_ROOT, (o1i - o1r) * HALF_ROOT)
        odd[2] = (o2i, -o2r)
        odd[3] = ((o3i - o3r) * HALF_ROOT, (-o3i - o3r) * HALF_ROOT)
    else:
        odd[1] = ((o1r - o1i) * HALF_ROOT, (o1i + o1r) * HALF_ROOT)
        odd[2] = (-o2i, o2r)
        odd[3] = ((-o3r - o3i) * HALF_ROOT, (o3r - o3i) * HALF_ROOT)
    low = [(e[0] + o[0], e[1] + o[1]) for e, o in zip(even, odd)]
    high = [(e[0] - o[0], e[1] - o[1]) for e, o in zip(even, odd)]
    return low + high


def store_split(high_ref, low_ref, index, value):
    high = value.astype(BF16)
    high_ref[index] = high
    low_ref[index] = (value - high.astype(F32)).astype(BF16)


def forward_blocks(source, half, mid, high_ref, low_ref, twiddle):
    for k2 in range(8):
        x = [source[half, k2 + 8 * k1].astype(F32) for k1 in range(4)]
        x0, x1, x2, x3 = x

        def real_times(value, angle):
            return value * float(np.cos(angle)), value * float(np.sin(angle))

        t1 = real_times(x1, -2 * np.pi / 16)
        t2 = real_times(x2, -2 * np.pi * 2 / 16)
        t3 = real_times(x3, -2 * np.pi * 3 / 16)
        er, ei, fr, fi = x0 + t2[0], t2[1], x0 - t2[0], -t2[1]
        gr, gi, hr, hi = t1[0] + t3[0], t1[1] + t3[1], t1[0] - t3[0], t1[1] - t3[1]
        results = [(er + gr, ei + gi), (fr + hi, fi - hr), (er - gr, ei - gi), (fr - hi, fi + hr)]
        for f1 in range(4):
            re, im = times(results[f1], -2 * np.pi * k2 * (0.25 + f1) / 32)
            mid[0, f1, k2] = re
            mid[1, f1, k2] = im
    for f1 in range(4):
        spectrum = fft8([(mid[0, f1, k2], mid[1, f1, k2]) for k2 in range(8)], -1)
        for f2 in range(8):
            f = f1 + 4 * f2
            c = twiddle[0, f : f + 1, :]
            s = twiddle[1, f : f + 1, :]
            re, im = spectrum[f2]
            rows = pl.ds(f * ROWS, ROWS)
            store_split(high_ref, low_ref, (rows, pl.ds(0, LANES)), re * c + im * s)
            store_split(high_ref, low_ref, (rows, pl.ds(LANES, LANES)), im * c - re * s)


def inverse_blocks(source, mid, out, half, twiddle, feature_q, skipped):
    for f1 in range(4):
        values = []
        for f2 in range(8):
            f = f1 + 4 * f2
            c = twiddle[0, f : f + 1, :]
            s = twiddle[1, f : f + 1, :]
            re = source[pl.ds(f * ROWS, ROWS), pl.ds(0, LANES)]
            im = source[pl.ds(f * ROWS, ROWS), pl.ds(LANES, LANES)]
            values.append((re * c - im * s, im * c + re * s))
        spectrum = fft8(values, 1)
        for k2 in range(8):
            re, im = times(spectrum[k2], 2 * np.pi * k2 * (0.25 + f1) / 32)
            mid[0, f1, k2] = re
            mid[1, f1, k2] = im
    for k2 in range(8):
        u = fft4([(mid[0, f1, k2], mid[1, f1, k2]) for f1 in range(4)], 1)
        for k1 in range(4):
            angle = 2 * np.pi * k1 / 16
            re, im = u[k1]
            y = re if k1 == 0 else re * float(np.cos(angle)) - im * float(np.sin(angle))
            k = k2 + 8 * k1
            out[half, k] = (feature_q[k] * (y + skipped[k])).astype(BF16)


def dot(a, b):
    return jnp.dot(a, b, preferred_element_type=F32)


CHUNK = 128
SPECTRUM_ROWS = BLOCKS * ROWS


def filter_spectrum(high_ref, low_ref, dft, out, half):
    def step(i, carry):
        rows = pl.ds(pl.multiple_of(i * CHUNK, CHUNK), CHUNK)
        high, low = high_ref[rows, :], low_ref[rows, :]
        out[half, rows, :] = dot(high, dft[0]) + dot(low, dft[0]) + dot(high, dft[1])
        return carry

    lax.fori_loop(0, SPECTRUM_ROWS // CHUNK, step, 0)


def multiply_spectra(high_ref, low_ref, dft, filters, half, out):
    def step(i, carry):
        rows = pl.ds(pl.multiple_of(i * CHUNK, CHUNK), CHUNK)
        high, low = high_ref[rows, :], low_ref[rows, :]
        g = dot(high, dft[0]) + dot(low, dft[0]) + dot(high, dft[1])
        h = filters[half, rows, :]
        gr, gi, hr, hi = g[:, :LANES], g[:, LANES:], h[:, :LANES], h[:, LANES:]
        product = jnp.concatenate([gr * hr - gi * hi, gr * hi + gi * hr], axis=1)
        high = product.astype(BF16)
        low = (product - high.astype(F32)).astype(BF16)
        out[rows, :] = dot(high, dft[2]) + dot(low, dft[2]) + dot(high, dft[3])
        return carry

    lax.fori_loop(0, SPECTRUM_ROWS // CHUNK, step, 0)


def kernel(
    q_hbm, k_hbm, v_hbm, fw_hbm, h_hbm, skip_hbm, w_hbm, tw_hbm, dft_hbm,
    out_ref,
    q_in, k_in, v_in, fw_ref, h_in, skip_ref, w_in, twiddle, dft,
    tails, halo, extended, columns, feature_q, skipped,
    h_send, g_send, q_send, m_send, h_all, g_all, q_all,
    mid, high_ref, low_ref, h_spec, v_spec, mixed, total, out_stage,
    local_sem, halo_sem, h_sem, g_sem, q_sem, m_sem, swap_sem, out_sem,
):
    n = lax.axis_size("seq")
    me = lax.axis_index("seq")
    mine = lax.axis_index("ch")
    across = lax.rem(mine + 2, 4)
    beside = mine + 1 - 2 * lax.rem(mine, 2)
    diagonal = lax.rem(beside + 2, 4)

    xs = [lax.rem(me // 8 + d, 4) * 8 for d in range(4)]
    ys = [lax.rem(me // 4 + d, 2) * 4 for d in range(2)]
    zs = [lax.rem(me + d, 4) for d in range(4)]
    peers = [xs[dx] + ys[dy] + zs[dz] for dx, dy, dz in FAR_FIRST]

    barrier = pltpu.get_barrier_semaphore()
    for peer in peers:
        pl.semaphore_signal(barrier, inc=1, device_id={"seq": peer}, device_id_type=MESH)
    for target in (across, beside):
        pl.semaphore_signal(barrier, inc=1, device_id={"ch": target}, device_id_type=MESH)

    pairs = [
        (k_hbm, k_in), (v_hbm, v_in), (q_hbm, q_in), (h_hbm, h_in), (fw_hbm, fw_ref), (skip_hbm, skip_ref),
        (tw_hbm, twiddle), (dft_hbm, dft), (w_hbm, w_in),
    ]
    local = [pltpu.make_async_copy(source, target, local_sem.at[i]) for i, (source, target) in enumerate(pairs)]
    for copy in local:
        copy.start()

    for i in range(3):
        local[i].wait()
    ends = [x[112:128, :].astype(F32)[14:16, :] for x in (k_in, v_in)]
    tails[...] = jnp.concatenate(ends * 2, axis=0)
    for i in range(3, 6):
        local[i].wait()

    def turned(block):
        return block.T.astype(BF16).reshape(TILES, ROWS, LANES)

    def place(i):
        return i * 128 // WIDTH, pl.ds(lax.rem(i * 128, WIDTH) // ROWS, TILES)

    def turn(i, carry):
        cols = pl.ds(pl.multiple_of(i * 128, 128), 128)
        part, blocks = place(i)
        h_send[part, blocks] = turned(h_in[:, cols])
        q_send[part, blocks] = turned(q_in[:, cols].astype(F32))
        rows = jnp.concatenate([skip_ref[0:1, cols], fw_ref[0, :, cols], jnp.zeros((124, 128), F32)], axis=0)
        columns[cols, :] = rows.T
        return carry

    lax.fori_loop(0, 8, turn, 0)

    pl.semaphore_wait(barrier, n - 1 + 2)

    halo_copy = pltpu.make_async_remote_copy(
        src_ref=tails, dst_ref=halo, send_sem=halo_sem.at[0], recv_sem=halo_sem.at[1],
        device_id={"seq": lax.rem(me + 1, n)}, device_id_type=MESH,
    )
    halo_copy.start()

    def scatter(source, target, part, sems):
        for peer in peers:
            pltpu.make_async_remote_copy(
                src_ref=source.at[part, peer], dst_ref=target.at[part, me],
                send_sem=sems.at[0, part], recv_sem=sems.at[1, part],
                device_id={"seq": peer}, device_id_type=MESH,
            ).start()
        target[part, me] = source[part, me]

    def all_of(ref, part, sems):
        view = ref.at[part, pl.ds(0, BLOCKS - 1)]
        return pltpu.make_async_remote_copy(
            src_ref=view, dst_ref=view, send_sem=sems.at[0, part], recv_sem=sems.at[1, part],
            device_id={"seq": lax.rem(me + 1, n)}, device_id_type=MESH,
        )

    def scatter_filters(part, carry):
        scatter(h_send, h_all, part, h_sem)
        return carry

    lax.fori_loop(0, PARTS, scatter_filters, 0)

    halo_copy.wait()
    keep = jnp.where(me == 0, 0.0, 1.0).astype(F32)
    for i, x in enumerate((k_in, v_in)):
        extended[i, 6:8, :] = halo[2 * i : 2 * i + 2, :] * keep

        def widen(r, carry):
            rows = pl.multiple_of(r * 16, 16)
            extended[i, pl.ds(rows + 8, 16), :] = x[pl.ds(rows, 16), :].astype(F32)
            return carry

        lax.fori_loop(0, 8, widen, 0)

    def feature(i, cols):
        result = fw_ref[i + 1, 0:1, cols] * extended[i, 8:136, cols]
        result += fw_ref[i + 1, 1:2, cols] * extended[i, 7:135, cols]
        return result + fw_ref[i + 1, 2:3, cols] * extended[i, 6:134, cols]

    def gate(i, carry):
        cols = pl.ds(pl.multiple_of(i * 128, 128), 128)
        part, blocks = place(i)
        g_send[part, blocks] = turned(feature(0, cols) * feature(1, cols))
        return carry

    def gate_part(part, carry):
        lax.fori_loop(part * (8 // PARTS), (part + 1) * (8 // PARTS), gate, 0)
        scatter(g_send, g_all, part, g_sem)
        scatter(q_send, q_all, part, q_sem)
        return carry

    lax.fori_loop(0, PARTS, gate_part, 0)

    local[6].wait()
    local[7].wait()

    def filters(part, carry):
        all_of(h_all, part, h_sem).wait_recv()
        forward_blocks(h_all, part, mid, high_ref, low_ref, twiddle)
        filter_spectrum(high_ref, low_ref, dft, h_spec, part)
        return carry

    lax.fori_loop(0, PARTS, filters, 0)

    lane = lax.broadcasted_iota(jnp.int32, (ROWS, LANES), 1)

    def query_features(part):
        own = columns[pl.ds(pl.multiple_of(part * WIDTH + me * ROWS, ROWS), ROWS), :]
        gain, w0, w1, w2 = [jnp.broadcast_to(own[:, i : i + 1], (ROWS, LANES)) for i in range(4)]
        before1 = before2 = jnp.zeros((ROWS, LANES), F32)
        for k in range(BLOCKS):
            x = q_all[part, k].astype(F32)
            now1, now2 = pltpu.roll(x, 1, 1), pltpu.roll(x, 2, 1)
            shifted = w1 * jnp.where(lane < 1, before1, now1) + w2 * jnp.where(lane < 2, before2, now2)
            feature_q[k] = w0 * x + shifted
            skipped[k] = gain * g_all[part, k].astype(F32)
            before1, before2 = now1, now2

    def convolve(part, carry):
        all_of(g_all, part, g_sem).wait_recv()
        forward_blocks(g_all, part, mid, high_ref, low_ref, twiddle)
        multiply_spectra(high_ref, low_ref, dft, h_spec, part, v_spec)
        all_of(q_all, part, q_sem).wait_recv()
        query_features(part)
        inverse_blocks(v_spec, mid, m_send, part, twiddle, feature_q, skipped)
        for peer in peers + [me]:
            for side, target in ((1, across), (0, mine)):
                if side == 0 and peer is me:
                    continue
                pltpu.make_async_remote_copy(
                    src_ref=m_send.at[part, peer], dst_ref=mixed.at[mine, part, me],
                    send_sem=m_sem.at[0, side, part], recv_sem=m_sem.at[1, side, part],
                    device_id={"seq": peer, "ch": target}, device_id_type=MESH,
                ).start()
        mixed[mine, part, me] = m_send[part, me]
        return carry

    lax.fori_loop(0, PARTS, convolve, 0)

    def arrived(side, part):
        view = mixed.at[0, part, pl.ds(0, BLOCKS - 1 + side)]
        return pltpu.make_async_remote_copy(
            src_ref=view, dst_ref=view, send_sem=m_sem.at[0, side, part], recv_sem=m_sem.at[1, side, part],
            device_id={"ch": across}, device_id_type=MESH,
        )

    def swap(slot, side, part):
        return pltpu.make_async_remote_copy(
            src_ref=mixed.at[slot, part], dst_ref=mixed.at[slot, part],
            send_sem=swap_sem.at[0, side, part], recv_sem=swap_sem.at[1, side, part],
            device_id={"ch": beside}, device_id_type=MESH,
        )

    def product(tokens, slot, part, cols):
        rows = pl.ds(pl.multiple_of(slot * 1024 + part * WIDTH, WIDTH), WIDTH)
        return dot(tokens, w_in[rows, cols])

    def by_token(slot, part):
        return mixed[slot, part].reshape(WIDTH, LANES).astype(F32).T.astype(BF16)

    def project(slot, part):
        tokens = by_token(slot, part)

        def step(j, carry):
            cols = pl.ds(pl.multiple_of(j * 256, 256), 256)
            total[:, cols] = total[:, cols] + product(tokens, slot, part, cols)
            return carry

        lax.fori_loop(0, 4, step, 0)

    total[...] = jnp.zeros_like(total)
    local[8].wait()
    for part in range(PARTS):
        arrived(0, part).wait_recv()
        swap(mine, 0, part).start()
        project(mine, part)
        arrived(1, part).wait_recv()
        swap(across, 1, part).start()
        project(across, part)
        swap(beside, 0, part).wait_recv()
        project(beside, part)
        swap(diagonal, 1, part).wait_recv()
        if part < PARTS - 1:
            project(diagonal, part)
    tokens = by_token(diagonal, PARTS - 1)

    def finish(j):
        cols = pl.ds(pl.multiple_of(j * 256, 256), 256)
        return pltpu.make_async_copy(out_stage.at[:, cols], out_ref.at[:, cols], out_sem.at[j])

    def last(j, carry):
        cols = pl.ds(pl.multiple_of(j * 256, 256), 256)
        out_stage[:, cols] = (total[:, cols] + product(tokens, diagonal, PARTS - 1, cols)).astype(BF16)
        finish(j).start()
        return carry

    lax.fori_loop(0, 4, last, 0)

    for part in range(PARTS):
        all_of(h_all, part, h_sem).wait_send()
        all_of(g_all, part, g_sem).wait_send()
        all_of(q_all, part, q_sem).wait_send()
        for side in range(2):
            arrived(side, part).wait_send()
            swap(mine, side, part).wait_send()
    for j in range(4):
        finish(j).wait()


def shards(query_proj, key_proj, value_proj, feat_weight, long_filter, skip_gain, out_weight):
    twiddle, dft = tables()
    anywhere = pl.BlockSpec(memory_space=pl.ANY)
    tokens, channels = query_proj.shape
    spectrum = (SPECTRUM_ROWS, 2 * LANES)
    turned = (PARTS, BLOCKS, ROWS, LANES)
    return pl.pallas_call(
        kernel,
        out_shape=jax.ShapeDtypeStruct((tokens, channels), BF16),
        in_specs=[anywhere] * 9,
        out_specs=anywhere,
        scratch_shapes=[
            pltpu.VMEM((tokens, channels), BF16),
            pltpu.VMEM((tokens, channels), BF16),
            pltpu.VMEM((tokens, channels), BF16),
            pltpu.VMEM(feat_weight.shape, F32),
            pltpu.VMEM((tokens, channels), F32),
            pltpu.VMEM((1, channels), F32),
            pltpu.VMEM(out_weight.shape, BF16),
            pltpu.VMEM(twiddle.shape, F32),
            pltpu.VMEM(dft.shape, BF16),
            pltpu.VMEM((8, channels), F32),
            pltpu.VMEM((8, channels), F32),
            pltpu.VMEM((2, tokens + 8, channels), F32),
            pltpu.VMEM((channels, LANES), F32),
            pltpu.VMEM((BLOCKS, ROWS, LANES), F32),
            pltpu.VMEM((BLOCKS, ROWS, LANES), F32),
            pltpu.VMEM(turned, BF16),
            pltpu.VMEM(turned, BF16),
            pltpu.VMEM(turned, BF16),
            pltpu.VMEM(turned, BF16),
            pltpu.VMEM(turned, BF16),
            pltpu.VMEM(turned, BF16),
            pltpu.VMEM(turned, BF16),
            pltpu.VMEM((2, 4, 8, ROWS, LANES), F32),
            pltpu.VMEM(spectrum, BF16),
            pltpu.VMEM(spectrum, BF16),
            pltpu.VMEM((PARTS,) + spectrum, F32),
            pltpu.VMEM(spectrum, F32),
            pltpu.VMEM((4,) + turned, BF16),
            pltpu.VMEM((tokens, channels), F32),
            pltpu.VMEM((tokens, channels), BF16),
            pltpu.SemaphoreType.DMA((9,)),
            pltpu.SemaphoreType.DMA((2,)),
            pltpu.SemaphoreType.DMA((2, PARTS)),
            pltpu.SemaphoreType.DMA((2, PARTS)),
            pltpu.SemaphoreType.DMA((2, PARTS)),
            pltpu.SemaphoreType.DMA((2, 2, PARTS)),
            pltpu.SemaphoreType.DMA((2, 2, PARTS)),
            pltpu.SemaphoreType.DMA((4,)),
        ],
        compiler_params=pltpu.CompilerParams(
            collective_id=0, has_side_effects=True, vmem_limit_bytes=56 * 1024 * 1024
        ),
        name="mixer",
    )(
        query_proj, key_proj, value_proj, feat_weight, long_filter, skip_gain[None, :], out_weight, twiddle, dft,
    )


def solution(mesh):
    placed = (
        P("seq", "ch"),
        P("seq", "ch"),
        P("seq", "ch"),
        P(None, None, "ch"),
        P("seq", "ch"),
        P("ch"),
        P(None, "ch"),
    )
    return jax.shard_map(shards, mesh=mesh, in_specs=placed, out_specs=P("seq", "ch"), check_vma=False)
```

```python
import functools

import jax
import jax.numpy as jnp
import numpy as np
from jax import lax
from jax.experimental import pallas as pl
from jax.experimental.pallas import tpu as pltpu
from jax.sharding import PartitionSpec as P

F32 = jnp.float32
BF16 = jnp.bfloat16
MESH = pl.DeviceIdType.MESH
BLOCKS = 32
LANES = 128
PARTS = 2
ROWS = 32 // PARTS
WIDTH = BLOCKS * ROWS
TILES = 128 // ROWS
FAR_FIRST = sorted(
    ((dx, dy, dz) for dx in range(4) for dy in range(2) for dz in range(4) if dx + dy + dz),
    key=lambda d: -(min(d[0], 4 - d[0]) + d[1] + min(d[2], 4 - d[2])),
)
HALF_ROOT = float(np.sqrt(0.5))


def tables():
    lane = np.arange(LANES)
    theta = 2 * np.pi * (np.arange(BLOCKS)[:, None] + 0.25) * lane[None, :] / (BLOCKS * LANES)
    twiddle = np.stack([np.cos(theta), np.sin(theta)]).astype(np.float32)
    phase = 2 * np.pi * (lane[:, None] * lane[None, :] % LANES) / LANES
    c, s = np.cos(phase), np.sin(phase)
    forward = np.block([[c, -s], [s, c]])
    inverse = np.block([[c, s], [-s, c]]) / (BLOCKS * LANES)
    parts = []
    for matrix in (forward, inverse):
        high = matrix.astype(BF16)
        parts += [high, (matrix - high.astype(np.float64)).astype(BF16)]
    return jnp.asarray(twiddle), jnp.asarray(np.stack(parts))


def times(value, angle):
    re, im = value
    c, s = float(np.cos(angle)), float(np.sin(angle))
    if abs(angle) < 1e-12:
        return re, im
    return re * c - im * s, im * c + re * s


def fft4(x, sign):
    (ar, ai), (br, bi), (cr, ci), (dr, di) = x
    er, ei, fr, fi = ar + cr, ai + ci, ar - cr, ai - ci
    gr, gi, hr, hi = br + dr, bi + di, br - dr, bi - di
    if sign < 0:
        jr, ji = hi, -hr
    else:
        jr, ji = -hi, hr
    return [(er + gr, ei + gi), (fr + jr, fi + ji), (er - gr, ei - gi), (fr - jr, fi - ji)]


def fft8(x, sign):
    even = fft4(x[0::2], sign)
    odd = fft4(x[1::2], sign)
    o1r, o1i = odd[1]
    o2r, o2i = odd[2]
    o3r, o3i = odd[3]
    if sign < 0:
        odd[1] = ((o1r + o1i) * HALF_ROOT, (o1i - o1r) * HALF_ROOT)
        odd[2] = (o2i, -o2r)
        odd[3] = ((o3i - o3r) * HALF_ROOT, (-o3i - o3r) * HALF_ROOT)
    else:
        odd[1] = ((o1r - o1i) * HALF_ROOT, (o1i + o1r) * HALF_ROOT)
        odd[2] = (-o2i, o2r)
        odd[3] = ((-o3r - o3i) * HALF_ROOT, (o3r - o3i) * HALF_ROOT)
    low = [(e[0] + o[0], e[1] + o[1]) for e, o in zip(even, odd)]
    high = [(e[0] - o[0], e[1] - o[1]) for e, o in zip(even, odd)]
    return low + high


def store_split(high_ref, low_ref, index, value):
    high = value.astype(BF16)
    high_ref[index] = high
    low_ref[index] = (value - high.astype(F32)).astype(BF16)


def forward_blocks(source, half, mid, high_ref, low_ref, twiddle):
    for k2 in range(8):
        x = [source[half, k2 + 8 * k1].astype(F32) for k1 in range(4)]
        x0, x1, x2, x3 = x

        def real_times(value, angle):
            return value * float(np.cos(angle)), value * float(np.sin(angle))

        t1 = real_times(x1, -2 * np.pi / 16)
        t2 = real_times(x2, -2 * np.pi * 2 / 16)
        t3 = real_times(x3, -2 * np.pi * 3 / 16)
        er, ei, fr, fi = x0 + t2[0], t2[1], x0 - t2[0], -t2[1]
        gr, gi, hr, hi = t1[0] + t3[0], t1[1] + t3[1], t1[0] - t3[0], t1[1] - t3[1]
        results = [(er + gr, ei + gi), (fr + hi, fi - hr), (er - gr, ei - gi), (fr - hi, fi + hr)]
        for f1 in range(4):
            re, im = times(results[f1], -2 * np.pi * k2 * (0.25 + f1) / 32)
            mid[0, f1, k2] = re
            mid[1, f1, k2] = im
    for f1 in range(4):
        spectrum = fft8([(mid[0, f1, k2], mid[1, f1, k2]) for k2 in range(8)], -1)
        for f2 in range(8):
            f = f1 + 4 * f2
            c = twiddle[0, f : f + 1, :]
            s = twiddle[1, f : f + 1, :]
            re, im = spectrum[f2]
            rows = pl.ds(f * ROWS, ROWS)
            store_split(high_ref, low_ref, (rows, pl.ds(0, LANES)), re * c + im * s)
            store_split(high_ref, low_ref, (rows, pl.ds(LANES, LANES)), im * c - re * s)


def inverse_blocks(source, mid, out, half, twiddle, feature_q, skipped):
    for f1 in range(4):
        values = []
        for f2 in range(8):
            f = f1 + 4 * f2
            c = twiddle[0, f : f + 1, :]
            s = twiddle[1, f : f + 1, :]
            re = source[pl.ds(f * ROWS, ROWS), pl.ds(0, LANES)]
            im = source[pl.ds(f * ROWS, ROWS), pl.ds(LANES, LANES)]
            values.append((re * c - im * s, im * c + re * s))
        spectrum = fft8(values, 1)
        for k2 in range(8):
            re, im = times(spectrum[k2], 2 * np.pi * k2 * (0.25 + f1) / 32)
            mid[0, f1, k2] = re
            mid[1, f1, k2] = im
    for k2 in range(8):
        u = fft4([(mid[0, f1, k2], mid[1, f1, k2]) for f1 in range(4)], 1)
        for k1 in range(4):
            angle = 2 * np.pi * k1 / 16
            re, im = u[k1]
            y = re if k1 == 0 else re * float(np.cos(angle)) - im * float(np.sin(angle))
            k = k2 + 8 * k1
            out[half, k] = (feature_q[k] * (y + skipped[k])).astype(BF16)


def dot(a, b):
    return jnp.dot(a, b, preferred_element_type=F32)


CHUNK = 512
SPECTRUM_ROWS = BLOCKS * ROWS


def filter_spectrum(high_ref, low_ref, dft, out, half):
    def step(i, carry):
        rows = pl.ds(pl.multiple_of(i * CHUNK, CHUNK), CHUNK)
        high, low = high_ref[rows, :], low_ref[rows, :]
        out[half, rows, :] = dot(high, dft[0]) + dot(low, dft[0]) + dot(high, dft[1])
        return carry

    lax.fori_loop(0, SPECTRUM_ROWS // CHUNK, step, 0)


def multiply_spectra(high_ref, low_ref, dft, filters, half, out):
    def step(i, carry):
        rows = pl.ds(pl.multiple_of(i * CHUNK, CHUNK), CHUNK)
        high, low = high_ref[rows, :], low_ref[rows, :]
        g = dot(high, dft[0]) + dot(low, dft[0]) + dot(high, dft[1])
        h = filters[half, rows, :]
        gr, gi, hr, hi = g[:, :LANES], g[:, LANES:], h[:, :LANES], h[:, LANES:]
        product = jnp.concatenate([gr * hr - gi * hi, gr * hi + gi * hr], axis=1)
        high = product.astype(BF16)
        low = (product - high.astype(F32)).astype(BF16)
        out[rows, :] = dot(high, dft[2]) + dot(low, dft[2]) + dot(high, dft[3])
        return carry

    lax.fori_loop(0, SPECTRUM_ROWS // CHUNK, step, 0)


def kernel(
    q_hbm, k_hbm, v_hbm, fw_hbm, h_hbm, skip_hbm, w_hbm, tw_hbm, dft_hbm,
    out_ref,
    q_in, k_in, v_in, fw_ref, h_in, skip_ref, w_in, twiddle, dft,
    tails, halo, extended, columns, feature_q, skipped,
    h_send, g_send, q_send, m_send, h_all, g_all, q_all,
    mid, high_ref, low_ref, h_spec, v_spec, mixed, total, out_stage,
    local_sem, halo_sem, h_sem, g_sem, q_sem, m_sem, swap_sem, out_sem,
):
    n = lax.axis_size("seq")
    me = lax.axis_index("seq")
    mine = lax.axis_index("ch")
    across = lax.rem(mine + 2, 4)
    beside = mine + 1 - 2 * lax.rem(mine, 2)
    diagonal = lax.rem(beside + 2, 4)

    xs = [lax.rem(me // 8 + d, 4) * 8 for d in range(4)]
    ys = [lax.rem(me // 4 + d, 2) * 4 for d in range(2)]
    zs = [lax.rem(me + d, 4) for d in range(4)]
    peers = [xs[dx] + ys[dy] + zs[dz] for dx, dy, dz in FAR_FIRST]

    barrier = pltpu.get_barrier_semaphore()
    for peer in peers:
        pl.semaphore_signal(barrier, inc=1, device_id={"seq": peer}, device_id_type=MESH)
    for target in (across, beside):
        pl.semaphore_signal(barrier, inc=1, device_id={"ch": target}, device_id_type=MESH)

    pairs = [
        (k_hbm, k_in), (v_hbm, v_in), (q_hbm, q_in), (h_hbm, h_in), (fw_hbm, fw_ref), (skip_hbm, skip_ref),
        (tw_hbm, twiddle), (dft_hbm, dft), (w_hbm, w_in),
    ]
    local = [pltpu.make_async_copy(source, target, local_sem.at[i]) for i, (source, target) in enumerate(pairs)]
    for copy in local:
        copy.start()

    for i in range(3):
        local[i].wait()
    ends = [x[112:128, :].astype(F32)[14:16, :] for x in (k_in, v_in)]
    tails[...] = jnp.concatenate(ends, axis=0).astype(BF16)
    for i in range(3, 6):
        local[i].wait()

    def turned(block):
        return block.astype(BF16).T.reshape(TILES, ROWS, LANES)

    def place(i):
        return i * 128 // WIDTH, pl.ds(lax.rem(i * 128, WIDTH) // ROWS, TILES)

    def turn(i, carry):
        cols = pl.ds(pl.multiple_of(i * 128, 128), 128)
        part, blocks = place(i)
        h_send[part, blocks] = turned(h_in[:, cols])
        q_send[part, blocks] = turned(q_in[:, cols])
        return carry

    lax.fori_loop(0, 8, turn, 0)

    for i, x in enumerate((k_in, v_in)):

        def widen(r, carry):
            rows = pl.multiple_of(r * 16, 16)
            extended[i, pl.ds(rows + 8, 16), :] = x[pl.ds(rows, 16), :].astype(F32)
            return carry

        lax.fori_loop(0, 8, widen, 0)

    pl.semaphore_wait(barrier, n - 1 + 2)

    halo_copy = pltpu.make_async_remote_copy(
        src_ref=tails, dst_ref=halo, send_sem=halo_sem.at[0], recv_sem=halo_sem.at[1],
        device_id={"seq": lax.rem(me + 1, n)}, device_id_type=MESH,
    )
    halo_copy.start()

    def scatter(source, target, part, sems):
        for peer in peers:
            pltpu.make_async_remote_copy(
                src_ref=source.at[part, peer], dst_ref=target.at[part, me],
                send_sem=sems.at[0, part], recv_sem=sems.at[1, part],
                device_id={"seq": peer}, device_id_type=MESH,
            ).start()
        target[part, me] = source[part, me]

    def all_of(ref, part, sems):
        view = ref.at[part, pl.ds(0, BLOCKS - 1)]
        return pltpu.make_async_remote_copy(
            src_ref=view, dst_ref=view, send_sem=sems.at[0, part], recv_sem=sems.at[1, part],
            device_id={"seq": lax.rem(me + 1, n)}, device_id_type=MESH,
        )

    scatter(h_send, h_all, 0, h_sem)
    scatter(h_send, h_all, 1, h_sem)

    for i in range(8):
        cols = pl.ds(i * 128, 128)
        rows = jnp.concatenate([skip_ref[0:1, cols], fw_ref[0, :, cols], jnp.zeros((4, 128), F32)], axis=0)
        columns[cols, :] = rows.T

    halo_copy.wait()
    before = halo[...].astype(F32) * jnp.where(me == 0, 0.0, 1.0).astype(F32)
    for i in range(2):
        extended[i, 6:8, :] = before[2 * i : 2 * i + 2, :]

    def feature(i, cols):
        result = fw_ref[i + 1, 0:1, cols] * extended[i, 8:136, cols]
        result += fw_ref[i + 1, 1:2, cols] * extended[i, 7:135, cols]
        return result + fw_ref[i + 1, 2:3, cols] * extended[i, 6:134, cols]

    def gate(i, carry):
        cols = pl.ds(pl.multiple_of(i * 128, 128), 128)
        part, blocks = place(i)
        g_send[part, blocks] = turned(feature(0, cols) * feature(1, cols))
        return carry

    def gate_part(part, carry):
        lax.fori_loop(part * (8 // PARTS), (part + 1) * (8 // PARTS), gate, 0)
        scatter(g_send, g_all, part, g_sem)
        scatter(q_send, q_all, part, q_sem)
        return carry

    lax.fori_loop(0, PARTS, gate_part, 0)

    local[6].wait()
    local[7].wait()

    def filters(part, carry):
        all_of(h_all, part, h_sem).wait_recv()
        forward_blocks(h_all, part, mid, high_ref, low_ref, twiddle)
        filter_spectrum(high_ref, low_ref, dft, h_spec, part)
        return carry

    lax.fori_loop(0, PARTS, filters, 0)

    lane = lax.broadcasted_iota(jnp.int32, (ROWS, LANES), 1)

    def query_features(part):
        own = columns[pl.ds(pl.multiple_of(part * WIDTH + me * ROWS, ROWS), ROWS), :]
        gain, w0, w1, w2 = [jnp.broadcast_to(own[:, i : i + 1], (ROWS, LANES)) for i in range(4)]
        before1 = before2 = jnp.zeros((ROWS, LANES), F32)
        for k in range(BLOCKS):
            x = q_all[part, k].astype(F32)
            now1, now2 = pltpu.roll(x, 1, 1), pltpu.roll(x, 2, 1)
            shifted = w1 * jnp.where(lane < 1, before1, now1) + w2 * jnp.where(lane < 2, before2, now2)
            feature_q[k] = w0 * x + shifted
            skipped[k] = gain * g_all[part, k].astype(F32)
            before1, before2 = now1, now2

    def convolve(part, carry):
        all_of(g_all, part, g_sem).wait_recv()
        forward_blocks(g_all, part, mid, high_ref, low_ref, twiddle)
        multiply_spectra(high_ref, low_ref, dft, h_spec, part, v_spec)
        all_of(q_all, part, q_sem).wait_recv()
        query_features(part)
        inverse_blocks(v_spec, mid, m_send, part, twiddle, feature_q, skipped)
        for side, target in ((1, across), (0, mine)):
            for peer in peers + [me] * side:
                pltpu.make_async_remote_copy(
                    src_ref=m_send.at[part, peer], dst_ref=mixed.at[mine, part, me],
                    send_sem=m_sem.at[0, side, part], recv_sem=m_sem.at[1, side, part],
                    device_id={"seq": peer, "ch": target}, device_id_type=MESH,
                ).start()
        mixed[mine, part, me] = m_send[part, me]
        return carry

    lax.fori_loop(0, PARTS, convolve, 0)

    def arrived(side, part):
        view = mixed.at[0, part, pl.ds(0, BLOCKS - 1 + side)]
        return pltpu.make_async_remote_copy(
            src_ref=view, dst_ref=view, send_sem=m_sem.at[0, side, part], recv_sem=m_sem.at[1, side, part],
            device_id={"ch": across}, device_id_type=MESH,
        )

    def swap(slot, side, part):
        return pltpu.make_async_remote_copy(
            src_ref=mixed.at[slot, part], dst_ref=mixed.at[slot, part],
            send_sem=swap_sem.at[0, side, part], recv_sem=swap_sem.at[1, side, part],
            device_id={"ch": beside}, device_id_type=MESH,
        )

    def product(tokens, slot, part, cols):
        rows = pl.ds(pl.multiple_of(slot * 1024 + part * WIDTH, WIDTH), WIDTH)
        return dot(tokens, w_in[rows, cols])

    def by_token(slot, part):
        return mixed[slot, part].reshape(WIDTH, LANES).astype(F32).T.astype(BF16)

    def project(slot, part):
        tokens = by_token(slot, part)

        for j in range(4):
            cols = pl.ds(j * 256, 256)
            total[:, cols] = total[:, cols] + product(tokens, slot, part, cols)

    total[...] = jnp.zeros_like(total)
    local[8].wait()
    for part in range(PARTS):
        arrived(1, part).wait_recv()
        swap(across, 1, part).start()
        project(across, part)
        arrived(0, part).wait_recv()
        swap(mine, 0, part).start()
        project(mine, part)
        swap(beside, 0, part).wait_recv()
        project(beside, part)
        swap(diagonal, 1, part).wait_recv()
        if part < PARTS - 1:
            project(diagonal, part)
    tokens = by_token(diagonal, PARTS - 1)

    def finish(j):
        cols = pl.ds(j * 256, 256)
        return pltpu.make_async_copy(out_stage.at[:, cols], out_ref.at[:, cols], out_sem.at[j])

    for j in range(4):
        cols = pl.ds(j * 256, 256)
        out_stage[:, cols] = (total[:, cols] + product(tokens, diagonal, PARTS - 1, cols)).astype(BF16)
        finish(j).start()

    for part in range(PARTS):
        all_of(h_all, part, h_sem).wait_send()
        all_of(g_all, part, g_sem).wait_send()
        all_of(q_all, part, q_sem).wait_send()
        for side in range(2):
            arrived(side, part).wait_send()
            swap(mine, side, part).wait_send()
    for j in range(4):
        finish(j).wait()


def shards(query_proj, key_proj, value_proj, feat_weight, long_filter, skip_gain, out_weight):
    twiddle, dft = tables()
    anywhere = pl.BlockSpec(memory_space=pl.ANY)
    tokens, channels = query_proj.shape
    spectrum = (SPECTRUM_ROWS, 2 * LANES)
    turned = (PARTS, BLOCKS, ROWS, LANES)
    return pl.pallas_call(
        kernel,
        out_shape=jax.ShapeDtypeStruct((tokens, channels), BF16),
        in_specs=[anywhere] * 9,
        out_specs=anywhere,
        scratch_shapes=[
            pltpu.VMEM((tokens, channels), BF16),
            pltpu.VMEM((tokens, channels), BF16),
            pltpu.VMEM((tokens, channels), BF16),
            pltpu.VMEM(feat_weight.shape, F32),
            pltpu.VMEM((tokens, channels), F32),
            pltpu.VMEM((1, channels), F32),
            pltpu.VMEM(out_weight.shape, BF16),
            pltpu.VMEM(twiddle.shape, F32),
            pltpu.VMEM(dft.shape, BF16),
            pltpu.VMEM((4, channels), BF16),
            pltpu.VMEM((4, channels), BF16),
            pltpu.VMEM((2, tokens + 8, channels), F32),
            pltpu.VMEM((channels, 8), F32),
            pltpu.VMEM((BLOCKS, ROWS, LANES), F32),
            pltpu.VMEM((BLOCKS, ROWS, LANES), F32),
            pltpu.VMEM(turned, BF16),
            pltpu.VMEM(turned, BF16),
            pltpu.VMEM(turned, BF16),
            pltpu.VMEM(turned, BF16),
            pltpu.VMEM(turned, BF16),
            pltpu.VMEM(turned, BF16),
            pltpu.VMEM(turned, BF16),
            pltpu.VMEM((2, 4, 8, ROWS, LANES), F32),
            pltpu.VMEM(spectrum, BF16),
            pltpu.VMEM(spectrum, BF16),
            pltpu.VMEM((PARTS,) + spectrum, F32),
            pltpu.VMEM(spectrum, F32),
            pltpu.VMEM((4,) + turned, BF16),
            pltpu.VMEM((tokens, channels), F32),
            pltpu.VMEM((tokens, channels), BF16),
            pltpu.SemaphoreType.DMA((9,)),
            pltpu.SemaphoreType.DMA((2,)),
            pltpu.SemaphoreType.DMA((2, PARTS)),
            pltpu.SemaphoreType.DMA((2, PARTS)),
            pltpu.SemaphoreType.DMA((2, PARTS)),
            pltpu.SemaphoreType.DMA((2, 2, PARTS)),
            pltpu.SemaphoreType.DMA((2, 2, PARTS)),
            pltpu.SemaphoreType.DMA((4,)),
        ],
        compiler_params=pltpu.CompilerParams(
            collective_id=0, has_side_effects=True, vmem_limit_bytes=56 * 1024 * 1024
        ),
        name="mixer",
    )(
        query_proj, key_proj, value_proj, feat_weight, long_filter, skip_gain[None, :], out_weight, twiddle, dft,
    )


def solution(mesh):
    placed = (
        P("seq", "ch"),
        P("seq", "ch"),
        P("seq", "ch"),
        P(None, None, "ch"),
        P("seq", "ch"),
        P("ch"),
        P(None, "ch"),
    )
    return jax.shard_map(shards, mesh=mesh, in_specs=placed, out_specs=P("seq", "ch"), check_vma=False)
```

```python
import functools

import jax
import jax.numpy as jnp
import numpy as np
from jax import lax
from jax.experimental import pallas as pl
from jax.experimental.pallas import tpu as pltpu
from jax.sharding import PartitionSpec as P

F32 = jnp.float32
BF16 = jnp.bfloat16
MESH = pl.DeviceIdType.MESH
BLOCKS = 32
LANES = 128
PARTS = 2
ROWS = 32 // PARTS
WIDTH = BLOCKS * ROWS
TILES = 128 // ROWS
FAR_FIRST = sorted(
    ((dx, dy, dz) for dx in range(4) for dy in range(2) for dz in range(4) if dx + dy + dz),
    key=lambda d: -(min(d[0], 4 - d[0]) + d[1] + min(d[2], 4 - d[2])),
)
HALF_ROOT = float(np.sqrt(0.5))


def tables():
    lane = np.arange(LANES)
    theta = 2 * np.pi * (np.arange(BLOCKS)[:, None] + 0.25) * lane[None, :] / (BLOCKS * LANES)
    twiddle = np.stack([np.cos(theta), np.sin(theta)]).astype(np.float32)
    phase = 2 * np.pi * (lane[:, None] * lane[None, :] % LANES) / LANES
    c, s = np.cos(phase), np.sin(phase)
    forward = np.block([[c, -s], [s, c]])
    inverse = np.block([[c, s], [-s, c]]) / (BLOCKS * LANES)
    parts = []
    for matrix in (forward, inverse):
        high = matrix.astype(BF16)
        parts += [high, (matrix - high.astype(np.float64)).astype(BF16)]
    return jnp.asarray(twiddle), jnp.asarray(np.stack(parts))


def times(value, angle):
    re, im = value
    c, s = float(np.cos(angle)), float(np.sin(angle))
    if abs(angle) < 1e-12:
        return re, im
    return re * c - im * s, im * c + re * s


def fft4(x, sign):
    (ar, ai), (br, bi), (cr, ci), (dr, di) = x
    er, ei, fr, fi = ar + cr, ai + ci, ar - cr, ai - ci
    gr, gi, hr, hi = br + dr, bi + di, br - dr, bi - di
    if sign < 0:
        jr, ji = hi, -hr
    else:
        jr, ji = -hi, hr
    return [(er + gr, ei + gi), (fr + jr, fi + ji), (er - gr, ei - gi), (fr - jr, fi - ji)]


def fft8(x, sign):
    even = fft4(x[0::2], sign)
    odd = fft4(x[1::2], sign)
    o1r, o1i = odd[1]
    o2r, o2i = odd[2]
    o3r, o3i = odd[3]
    if sign < 0:
        odd[1] = ((o1r + o1i) * HALF_ROOT, (o1i - o1r) * HALF_ROOT)
        odd[2] = (o2i, -o2r)
        odd[3] = ((o3i - o3r) * HALF_ROOT, (-o3i - o3r) * HALF_ROOT)
    else:
        odd[1] = ((o1r - o1i) * HALF_ROOT, (o1i + o1r) * HALF_ROOT)
        odd[2] = (-o2i, o2r)
        odd[3] = ((-o3r - o3i) * HALF_ROOT, (o3r - o3i) * HALF_ROOT)
    low = [(e[0] + o[0], e[1] + o[1]) for e, o in zip(even, odd)]
    high = [(e[0] - o[0], e[1] - o[1]) for e, o in zip(even, odd)]
    return low + high


def store_split(high_ref, low_ref, index, value):
    high = value.astype(BF16)
    high_ref[index] = high
    low_ref[index] = (value - high.astype(F32)).astype(BF16)


def forward_blocks(source, half, mid, high_ref, low_ref, twiddle):
    for k2 in range(8):
        x = [source[half, k2 + 8 * k1].astype(F32) for k1 in range(4)]
        x0, x1, x2, x3 = x

        def real_times(value, angle):
            return value * float(np.cos(angle)), value * float(np.sin(angle))

        t1 = real_times(x1, -2 * np.pi / 16)
        t2 = real_times(x2, -2 * np.pi * 2 / 16)
        t3 = real_times(x3, -2 * np.pi * 3 / 16)
        er, ei, fr, fi = x0 + t2[0], t2[1], x0 - t2[0], -t2[1]
        gr, gi, hr, hi = t1[0] + t3[0], t1[1] + t3[1], t1[0] - t3[0], t1[1] - t3[1]
        results = [(er + gr, ei + gi), (fr + hi, fi - hr), (er - gr, ei - gi), (fr - hi, fi + hr)]
        for f1 in range(4):
            re, im = times(results[f1], -2 * np.pi * k2 * (0.25 + f1) / 32)
            mid[0, f1, k2] = re
            mid[1, f1, k2] = im
    for f1 in range(4):
        spectrum = fft8([(mid[0, f1, k2], mid[1, f1, k2]) for k2 in range(8)], -1)
        for f2 in range(8):
            f = f1 + 4 * f2
            c = twiddle[0, f : f + 1, :]
            s = twiddle[1, f : f + 1, :]
            re, im = spectrum[f2]
            rows = pl.ds(f * ROWS, ROWS)
            store_split(high_ref, low_ref, (rows, pl.ds(0, LANES)), re * c + im * s)
            store_split(high_ref, low_ref, (rows, pl.ds(LANES, LANES)), im * c - re * s)


def inverse_blocks(source, mid, out, half, twiddle, feature_q, gains, g_all):
    for f1 in range(4):
        values = []
        for f2 in range(8):
            f = f1 + 4 * f2
            c = twiddle[0, f : f + 1, :]
            s = twiddle[1, f : f + 1, :]
            re = source[pl.ds(f * ROWS, ROWS), pl.ds(0, LANES)]
            im = source[pl.ds(f * ROWS, ROWS), pl.ds(LANES, LANES)]
            values.append((re * c - im * s, im * c + re * s))
        spectrum = fft8(values, 1)
        for k2 in range(8):
            re, im = times(spectrum[k2], 2 * np.pi * k2 * (0.25 + f1) / 32)
            mid[0, f1, k2] = re
            mid[1, f1, k2] = im
    gain = gains[...]
    for k2 in range(8):
        u = fft4([(mid[0, f1, k2], mid[1, f1, k2]) for f1 in range(4)], 1)
        for k1 in range(4):
            angle = 2 * np.pi * k1 / 16
            re, im = u[k1]
            y = re if k1 == 0 else re * float(np.cos(angle)) - im * float(np.sin(angle))
            k = k2 + 8 * k1
            out[half, k] = (feature_q[k] * (y + gain * g_all[half, k].astype(F32))).astype(BF16)


def dot(a, b):
    return jnp.dot(a, b, preferred_element_type=F32)


CHUNK = 512
SPECTRUM_ROWS = BLOCKS * ROWS


def filter_spectrum(high_ref, low_ref, dft, out, half):
    def step(i, carry):
        rows = pl.ds(pl.multiple_of(i * CHUNK, CHUNK), CHUNK)
        high, low = high_ref[rows, :], low_ref[rows, :]
        out[half, rows, :] = dot(high, dft[0]) + dot(low, dft[0]) + dot(high, dft[1])
        return carry

    lax.fori_loop(0, SPECTRUM_ROWS // CHUNK, step, 0)


def multiply_spectra(high_ref, low_ref, dft, filters, half, out):
    def step(i, carry):
        rows = pl.ds(pl.multiple_of(i * CHUNK, CHUNK), CHUNK)
        high, low = high_ref[rows, :], low_ref[rows, :]
        g = dot(high, dft[0]) + dot(low, dft[0]) + dot(high, dft[1])
        h = filters[half, rows, :]
        gr, gi, hr, hi = g[:, :LANES], g[:, LANES:], h[:, :LANES], h[:, LANES:]
        product = jnp.concatenate([gr * hr - gi * hi, gr * hi + gi * hr], axis=1)
        high = product.astype(BF16)
        low = (product - high.astype(F32)).astype(BF16)
        out[rows, :] = dot(high, dft[2]) + dot(low, dft[2]) + dot(high, dft[3])
        return carry

    lax.fori_loop(0, SPECTRUM_ROWS // CHUNK, step, 0)


def kernel(
    q_hbm, k_hbm, v_hbm, fw_hbm, h_hbm, skip_hbm, w_hbm, tw_hbm, dft_hbm,
    out_ref,
    q_in, k_in, v_in, fw_ref, h_in, skip_ref, w_in, twiddle, dft,
    tails, halo, extended, columns, feature_q, gains,
    h_send, g_send, q_send, m_send, h_all, g_all, q_all,
    mid, high_ref, low_ref, h_spec, v_spec, mixed, total, out_stage,
    local_sem, halo_sem, h_sem, g_sem, q_sem, m_sem, swap_sem, out_sem,
):
    n = lax.axis_size("seq")
    me = lax.axis_index("seq")
    mine = lax.axis_index("ch")
    across = lax.rem(mine + 2, 4)
    beside = mine + 1 - 2 * lax.rem(mine, 2)
    diagonal = lax.rem(beside + 2, 4)

    xs = [lax.rem(me // 8 + d, 4) * 8 for d in range(4)]
    ys = [lax.rem(me // 4 + d, 2) * 4 for d in range(2)]
    zs = [lax.rem(me + d, 4) for d in range(4)]
    peers = [xs[dx] + ys[dy] + zs[dz] for dx, dy, dz in FAR_FIRST]

    barrier = pltpu.get_barrier_semaphore()
    for peer in peers:
        pl.semaphore_signal(barrier, inc=1, device_id={"seq": peer}, device_id_type=MESH)
    for target in (across, beside):
        pl.semaphore_signal(barrier, inc=1, device_id={"ch": target}, device_id_type=MESH)

    pairs = [
        (k_hbm, k_in), (v_hbm, v_in), (q_hbm, q_in), (h_hbm, h_in), (fw_hbm, fw_ref), (skip_hbm, skip_ref),
        (tw_hbm, twiddle), (dft_hbm, dft), (w_hbm, w_in),
    ]
    local = [pltpu.make_async_copy(source, target, local_sem.at[i]) for i, (source, target) in enumerate(pairs)]
    for copy in local:
        copy.start()

    for i in range(3):
        local[i].wait()
    ends = [x[112:128, :].astype(F32)[14:16, :] for x in (k_in, v_in)]
    tails[...] = jnp.concatenate(ends, axis=0).astype(BF16)
    for i in range(3, 6):
        local[i].wait()

    def turned(block):
        return block.astype(BF16).T.reshape(TILES, ROWS, LANES)

    def place(i):
        return i * 128 // WIDTH, pl.ds(lax.rem(i * 128, WIDTH) // ROWS, TILES)

    def turn(i, carry):
        cols = pl.ds(pl.multiple_of(i * 128, 128), 128)
        part, blocks = place(i)
        h_send[part, blocks] = turned(h_in[:, cols])
        q_send[part, blocks] = turned(q_in[:, cols])
        return carry

    lax.fori_loop(0, 8, turn, 0)

    for i, x in enumerate((k_in, v_in)):

        def widen(r, carry):
            rows = pl.multiple_of(r * 16, 16)
            extended[i, pl.ds(rows + 8, 16), :] = x[pl.ds(rows, 16), :].astype(F32)
            return carry

        lax.fori_loop(0, 8, widen, 0)

    pl.semaphore_wait(barrier, n - 1 + 2)

    halo_copy = pltpu.make_async_remote_copy(
        src_ref=tails, dst_ref=halo, send_sem=halo_sem.at[0], recv_sem=halo_sem.at[1],
        device_id={"seq": lax.rem(me + 1, n)}, device_id_type=MESH,
    )
    halo_copy.start()

    def scatter(source, target, part, sems):
        for peer in peers:
            pltpu.make_async_remote_copy(
                src_ref=source.at[part, peer], dst_ref=target.at[part, me],
                send_sem=sems.at[0, part], recv_sem=sems.at[1, part],
                device_id={"seq": peer}, device_id_type=MESH,
            ).start()
        target[part, me] = source[part, me]

    def all_of(ref, part, sems):
        view = ref.at[part, pl.ds(0, BLOCKS - 1)]
        return pltpu.make_async_remote_copy(
            src_ref=view, dst_ref=view, send_sem=sems.at[0, part], recv_sem=sems.at[1, part],
            device_id={"seq": lax.rem(me + 1, n)}, device_id_type=MESH,
        )

    scatter(h_send, h_all, 0, h_sem)
    scatter(h_send, h_all, 1, h_sem)

    for i in range(8):
        cols = pl.ds(i * 128, 128)
        rows = jnp.concatenate([skip_ref[0:1, cols], fw_ref[0, :, cols], jnp.zeros((4, 128), F32)], axis=0)
        columns[cols, :] = rows.T

    halo_copy.wait()
    before = halo[...].astype(F32) * jnp.where(me == 0, 0.0, 1.0).astype(F32)
    for i in range(2):
        extended[i, 6:8, :] = before[2 * i : 2 * i + 2, :]

    def feature(i, cols):
        result = fw_ref[i + 1, 0:1, cols] * extended[i, 8:136, cols]
        result += fw_ref[i + 1, 1:2, cols] * extended[i, 7:135, cols]
        return result + fw_ref[i + 1, 2:3, cols] * extended[i, 6:134, cols]

    def gate(i, carry):
        cols = pl.ds(pl.multiple_of(i * 128, 128), 128)
        part, blocks = place(i)
        g_send[part, blocks] = turned(feature(0, cols) * feature(1, cols))
        return carry

    def gate_part(part, carry):
        lax.fori_loop(part * (8 // PARTS), (part + 1) * (8 // PARTS), gate, 0)
        scatter(g_send, g_all, part, g_sem)
        scatter(q_send, q_all, part, q_sem)
        return carry

    lax.fori_loop(0, PARTS, gate_part, 0)

    local[6].wait()
    local[7].wait()

    def filters(part, carry):
        all_of(h_all, part, h_sem).wait_recv()
        forward_blocks(h_all, part, mid, high_ref, low_ref, twiddle)
        filter_spectrum(high_ref, low_ref, dft, h_spec, part)
        return carry

    lax.fori_loop(0, PARTS, filters, 0)

    lane = lax.broadcasted_iota(jnp.int32, (ROWS, LANES), 1)

    def query_features(part):
        own = columns[pl.ds(pl.multiple_of(part * WIDTH + me * ROWS, ROWS), ROWS), :]
        w0, w1, w2 = [jnp.broadcast_to(own[:, i : i + 1], (ROWS, LANES)) for i in range(1, 4)]
        gains[...] = jnp.broadcast_to(own[:, 0:1], (ROWS, LANES))
        before1 = before2 = jnp.zeros((ROWS, LANES), F32)
        for k in range(BLOCKS):
            x = q_all[part, k].astype(F32)
            now1, now2 = pltpu.roll(x, 1, 1), pltpu.roll(x, 2, 1)
            shifted = w1 * jnp.where(lane < 1, before1, now1) + w2 * jnp.where(lane < 2, before2, now2)
            feature_q[k] = w0 * x + shifted
            before1, before2 = now1, now2

    def convolve(part, carry):
        all_of(g_all, part, g_sem).wait_recv()
        forward_blocks(g_all, part, mid, high_ref, low_ref, twiddle)
        multiply_spectra(high_ref, low_ref, dft, h_spec, part, v_spec)
        all_of(q_all, part, q_sem).wait_recv()
        query_features(part)
        inverse_blocks(v_spec, mid, m_send, part, twiddle, feature_q, gains, g_all)
        for side, target in ((1, across), (0, mine)):
            for peer in peers + [me] * side:
                pltpu.make_async_remote_copy(
                    src_ref=m_send.at[part, peer], dst_ref=mixed.at[mine, part, me],
                    send_sem=m_sem.at[0, side, part], recv_sem=m_sem.at[1, side, part],
                    device_id={"seq": peer, "ch": target}, device_id_type=MESH,
                ).start()
        mixed[mine, part, me] = m_send[part, me]
        return carry

    lax.fori_loop(0, PARTS, convolve, 0)

    def arrived(side, part):
        view = mixed.at[0, part, pl.ds(0, BLOCKS - 1 + side)]
        return pltpu.make_async_remote_copy(
            src_ref=view, dst_ref=view, send_sem=m_sem.at[0, side, part], recv_sem=m_sem.at[1, side, part],
            device_id={"ch": across}, device_id_type=MESH,
        )

    def swap(slot, side, part):
        return pltpu.make_async_remote_copy(
            src_ref=mixed.at[slot, part], dst_ref=mixed.at[slot, part],
            send_sem=swap_sem.at[0, side, part], recv_sem=swap_sem.at[1, side, part],
            device_id={"ch": beside}, device_id_type=MESH,
        )

    def product(tokens, slot, part, cols):
        rows = pl.ds(pl.multiple_of(slot * 1024 + part * WIDTH, WIDTH), WIDTH)
        return dot(tokens, w_in[rows, cols])

    def by_token(slot, part):
        return mixed[slot, part].reshape(WIDTH, LANES).T

    def project(slot, part):
        tokens = by_token(slot, part)

        for j in range(4):
            cols = pl.ds(j * 256, 256)
            total[:, cols] = total[:, cols] + product(tokens, slot, part, cols)

    total[...] = jnp.zeros_like(total)
    local[8].wait()
    for part in range(PARTS):
        arrived(1, part).wait_recv()
        swap(across, 1, part).start()
        project(across, part)
        arrived(0, part).wait_recv()
        swap(mine, 0, part).start()
        project(mine, part)
        swap(diagonal, 1, part).wait_recv()
        project(diagonal, part)
        swap(beside, 0, part).wait_recv()
        if part < PARTS - 1:
            project(beside, part)
    tokens = by_token(beside, PARTS - 1)

    def finish(j):
        cols = pl.ds(j * 256, 256)
        return pltpu.make_async_copy(out_stage.at[:, cols], out_ref.at[:, cols], out_sem.at[j])

    for j in range(4):
        cols = pl.ds(j * 256, 256)
        out_stage[:, cols] = (total[:, cols] + product(tokens, beside, PARTS - 1, cols)).astype(BF16)
        finish(j).start()

    for part in range(PARTS):
        all_of(h_all, part, h_sem).wait_send()
        all_of(g_all, part, g_sem).wait_send()
        all_of(q_all, part, q_sem).wait_send()
        for side in range(2):
            arrived(side, part).wait_send()
            swap(mine, side, part).wait_send()
    for j in range(4):
        finish(j).wait()


def shards(query_proj, key_proj, value_proj, feat_weight, long_filter, skip_gain, out_weight):
    twiddle, dft = tables()
    anywhere = pl.BlockSpec(memory_space=pl.ANY)
    tokens, channels = query_proj.shape
    spectrum = (SPECTRUM_ROWS, 2 * LANES)
    turned = (PARTS, BLOCKS, ROWS, LANES)
    return pl.pallas_call(
        kernel,
        out_shape=jax.ShapeDtypeStruct((tokens, channels), BF16),
        in_specs=[anywhere] * 9,
        out_specs=anywhere,
        scratch_shapes=[
            pltpu.VMEM((tokens, channels), BF16),
            pltpu.VMEM((tokens, channels), BF16),
            pltpu.VMEM((tokens, channels), BF16),
            pltpu.VMEM(feat_weight.shape, F32),
            pltpu.VMEM((tokens, channels), F32),
            pltpu.VMEM((1, channels), F32),
            pltpu.VMEM(out_weight.shape, BF16),
            pltpu.VMEM(twiddle.shape, F32),
            pltpu.VMEM(dft.shape, BF16),
            pltpu.VMEM((4, channels), BF16),
            pltpu.VMEM((4, channels), BF16),
            pltpu.VMEM((2, tokens + 8, channels), F32),
            pltpu.VMEM((channels, 8), F32),
            pltpu.VMEM((BLOCKS, ROWS, LANES), F32),
            pltpu.VMEM((ROWS, LANES), F32),
            pltpu.VMEM(turned, BF16),
            pltpu.VMEM(turned, BF16),
            pltpu.VMEM(turned, BF16),
            pltpu.VMEM(turned, BF16),
            pltpu.VMEM(turned, BF16),
            pltpu.VMEM(turned, BF16),
            pltpu.VMEM(turned, BF16),
            pltpu.VMEM((2, 4, 8, ROWS, LANES), F32),
            pltpu.VMEM(spectrum, BF16),
            pltpu.VMEM(spectrum, BF16),
            pltpu.VMEM((PARTS,) + spectrum, F32),
            pltpu.VMEM(spectrum, F32),
            pltpu.VMEM((4,) + turned, BF16),
            pltpu.VMEM((tokens, channels), F32),
            pltpu.VMEM((tokens, channels), BF16),
            pltpu.SemaphoreType.DMA((9,)),
            pltpu.SemaphoreType.DMA((2,)),
            pltpu.SemaphoreType.DMA((2, PARTS)),
            pltpu.SemaphoreType.DMA((2, PARTS)),
            pltpu.SemaphoreType.DMA((2, PARTS)),
            pltpu.SemaphoreType.DMA((2, 2, PARTS)),
            pltpu.SemaphoreType.DMA((2, 2, PARTS)),
            pltpu.SemaphoreType.DMA((4,)),
        ],
        compiler_params=pltpu.CompilerParams(
            collective_id=0, has_side_effects=True, vmem_limit_bytes=56 * 1024 * 1024
        ),
        name="mixer",
    )(
        query_proj, key_proj, value_proj, feat_weight, long_filter, skip_gain[None, :], out_weight, twiddle, dft,
    )


def solution(mesh):
    placed = (
        P("seq", "ch"),
        P("seq", "ch"),
        P("seq", "ch"),
        P(None, None, "ch"),
        P("seq", "ch"),
        P("ch"),
        P(None, "ch"),
    )
    return jax.shard_map(shards, mesh=mesh, in_specs=placed, out_specs=P("seq", "ch"), check_vma=False)
```

```python
import functools

import jax
import jax.numpy as jnp
import numpy as np
from jax import lax
from jax.experimental import pallas as pl
from jax.experimental.pallas import tpu as pltpu
from jax.sharding import PartitionSpec as P

F32 = jnp.float32
BF16 = jnp.bfloat16
MESH = pl.DeviceIdType.MESH
BLOCKS = 32
LANES = 128
PARTS = 2
ROWS = 32 // PARTS
WIDTH = BLOCKS * ROWS
TILES = 128 // ROWS
FAR_FIRST = sorted(
    ((dx, dy, dz) for dx in range(4) for dy in range(2) for dz in range(4) if dx + dy + dz),
    key=lambda d: -(min(d[0], 4 - d[0]) + d[1] + min(d[2], 4 - d[2])),
)
HALF_ROOT = float(np.sqrt(0.5))


def tables():
    lane = np.arange(LANES)
    theta = 2 * np.pi * (np.arange(BLOCKS)[:, None] + 0.25) * lane[None, :] / (BLOCKS * LANES)
    twiddle = np.stack([np.cos(theta), np.sin(theta)]).astype(np.float32)
    phase = 2 * np.pi * (lane[:, None] * lane[None, :] % LANES) / LANES
    c, s = np.cos(phase), np.sin(phase)
    forward = np.block([[c, -s], [s, c]])
    inverse = np.block([[c, s], [-s, c]]) / (BLOCKS * LANES)
    parts = []
    for matrix in (forward, inverse):
        high = matrix.astype(BF16)
        parts += [high, (matrix - high.astype(np.float64)).astype(BF16)]
    return jnp.asarray(twiddle), jnp.asarray(np.stack(parts))


def times(value, angle):
    re, im = value
    c, s = float(np.cos(angle)), float(np.sin(angle))
    if abs(angle) < 1e-12:
        return re, im
    return re * c - im * s, im * c + re * s


def fft4(x, sign):
    (ar, ai), (br, bi), (cr, ci), (dr, di) = x
    er, ei, fr, fi = ar + cr, ai + ci, ar - cr, ai - ci
    gr, gi, hr, hi = br + dr, bi + di, br - dr, bi - di
    if sign < 0:
        jr, ji = hi, -hr
    else:
        jr, ji = -hi, hr
    return [(er + gr, ei + gi), (fr + jr, fi + ji), (er - gr, ei - gi), (fr - jr, fi - ji)]


def fft8(x, sign):
    even = fft4(x[0::2], sign)
    odd = fft4(x[1::2], sign)
    o1r, o1i = odd[1]
    o2r, o2i = odd[2]
    o3r, o3i = odd[3]
    if sign < 0:
        odd[1] = ((o1r + o1i) * HALF_ROOT, (o1i - o1r) * HALF_ROOT)
        odd[2] = (o2i, -o2r)
        odd[3] = ((o3i - o3r) * HALF_ROOT, (-o3i - o3r) * HALF_ROOT)
    else:
        odd[1] = ((o1r - o1i) * HALF_ROOT, (o1i + o1r) * HALF_ROOT)
        odd[2] = (-o2i, o2r)
        odd[3] = ((-o3r - o3i) * HALF_ROOT, (o3r - o3i) * HALF_ROOT)
    low = [(e[0] + o[0], e[1] + o[1]) for e, o in zip(even, odd)]
    high = [(e[0] - o[0], e[1] - o[1]) for e, o in zip(even, odd)]
    return low + high


def store_split(high_ref, low_ref, index, value):
    high = value.astype(BF16)
    high_ref[index] = high
    low_ref[index] = (value - high.astype(F32)).astype(BF16)


def forward_blocks(source, half, mid, high_ref, low_ref, twiddle):
    for k2 in range(8):
        x = [source[half, k2 + 8 * k1].astype(F32) for k1 in range(4)]
        x0, x1, x2, x3 = x

        def real_times(value, angle):
            return value * float(np.cos(angle)), value * float(np.sin(angle))

        t1 = real_times(x1, -2 * np.pi / 16)
        t2 = real_times(x2, -2 * np.pi * 2 / 16)
        t3 = real_times(x3, -2 * np.pi * 3 / 16)
        er, ei, fr, fi = x0 + t2[0], t2[1], x0 - t2[0], -t2[1]
        gr, gi, hr, hi = t1[0] + t3[0], t1[1] + t3[1], t1[0] - t3[0], t1[1] - t3[1]
        results = [(er + gr, ei + gi), (fr + hi, fi - hr), (er - gr, ei - gi), (fr - hi, fi + hr)]
        for f1 in range(4):
            re, im = times(results[f1], -2 * np.pi * k2 * (0.25 + f1) / 32)
            mid[0, f1, k2] = re
            mid[1, f1, k2] = im
    for f1 in range(4):
        spectrum = fft8([(mid[0, f1, k2], mid[1, f1, k2]) for k2 in range(8)], -1)
        for f2 in range(8):
            f = f1 + 4 * f2
            c = twiddle[0, f : f + 1, :]
            s = twiddle[1, f : f + 1, :]
            re, im = spectrum[f2]
            rows = pl.ds(f * ROWS, ROWS)
            store_split(high_ref, low_ref, (rows, pl.ds(0, LANES)), re * c + im * s)
            store_split(high_ref, low_ref, (rows, pl.ds(LANES, LANES)), im * c - re * s)


def inverse_blocks(source, mid, out, half, twiddle, feature_q, gains, g_all):
    for f1 in range(4):
        values = []
        for f2 in range(8):
            f = f1 + 4 * f2
            c = twiddle[0, f : f + 1, :]
            s = twiddle[1, f : f + 1, :]
            re = source[pl.ds(f * ROWS, ROWS), pl.ds(0, LANES)]
            im = source[pl.ds(f * ROWS, ROWS), pl.ds(LANES, LANES)]
            values.append((re * c - im * s, im * c + re * s))
        spectrum = fft8(values, 1)
        for k2 in range(8):
            re, im = times(spectrum[k2], 2 * np.pi * k2 * (0.25 + f1) / 32)
            mid[0, f1, k2] = re
            mid[1, f1, k2] = im
    gain = gains[...]
    for k2 in range(8):
        u = fft4([(mid[0, f1, k2], mid[1, f1, k2]) for f1 in range(4)], 1)
        for k1 in range(4):
            angle = 2 * np.pi * k1 / 16
            re, im = u[k1]
            y = re if k1 == 0 else re * float(np.cos(angle)) - im * float(np.sin(angle))
            k = k2 + 8 * k1
            out[half, k] = (feature_q[k] * (y + gain * g_all[half, k].astype(F32))).astype(BF16)


def dot(a, b):
    return jnp.dot(a, b, preferred_element_type=F32)


CHUNK = 512
SPECTRUM_ROWS = BLOCKS * ROWS


def filter_spectrum(high_ref, low_ref, dft, out, half):
    def step(i, carry):
        rows = pl.ds(pl.multiple_of(i * CHUNK, CHUNK), CHUNK)
        high, low = high_ref[rows, :], low_ref[rows, :]
        out[half, rows, :] = dot(high, dft[0]) + dot(low, dft[0]) + dot(high, dft[1])
        return carry

    lax.fori_loop(0, SPECTRUM_ROWS // CHUNK, step, 0)


def multiply_spectra(high_ref, low_ref, dft, filters, half, out):
    def step(i, carry):
        rows = pl.ds(pl.multiple_of(i * CHUNK, CHUNK), CHUNK)
        high, low = high_ref[rows, :], low_ref[rows, :]
        g = dot(high, dft[0]) + dot(low, dft[0]) + dot(high, dft[1])
        h = filters[half, rows, :]
        gr, gi, hr, hi = g[:, :LANES], g[:, LANES:], h[:, :LANES], h[:, LANES:]
        product = jnp.concatenate([gr * hr - gi * hi, gr * hi + gi * hr], axis=1)
        high = product.astype(BF16)
        low = (product - high.astype(F32)).astype(BF16)
        out[rows, :] = dot(high, dft[2]) + dot(low, dft[2]) + dot(high, dft[3])
        return carry

    lax.fori_loop(0, SPECTRUM_ROWS // CHUNK, step, 0)


def kernel(
    q_hbm, k_hbm, v_hbm, fw_hbm, h_hbm, skip_hbm, w_hbm, tw_hbm, dft_hbm,
    out_ref,
    q_in, k_in, v_in, fw_ref, h_in, skip_ref, w_in, twiddle, dft,
    tails, halo, extended, columns, feature_q, gains,
    h_send, g_send, q_send, m_send, h_all, g_all, q_all,
    mid, high_ref, low_ref, h_spec, v_spec, mixed, total, out_stage,
    local_sem, halo_sem, h_sem, g_sem, q_sem, m_sem, swap_sem, out_sem,
):
    n = lax.axis_size("seq")
    me = lax.axis_index("seq")
    mine = lax.axis_index("ch")
    across = lax.rem(mine + 2, 4)
    beside = mine + 1 - 2 * lax.rem(mine, 2)
    diagonal = lax.rem(beside + 2, 4)

    xs = [lax.rem(me // 8 + d, 4) * 8 for d in range(4)]
    ys = [lax.rem(me // 4 + d, 2) * 4 for d in range(2)]
    zs = [lax.rem(me + d, 4) for d in range(4)]
    peers = [xs[dx] + ys[dy] + zs[dz] for dx, dy, dz in FAR_FIRST]

    barrier = pltpu.get_barrier_semaphore()
    for peer in peers:
        pl.semaphore_signal(barrier, inc=1, device_id={"seq": peer}, device_id_type=MESH)
    for target in (across, beside):
        pl.semaphore_signal(barrier, inc=1, device_id={"ch": target}, device_id_type=MESH)

    pairs = [
        (k_hbm, k_in), (v_hbm, v_in), (q_hbm, q_in), (h_hbm, h_in), (fw_hbm, fw_ref), (skip_hbm, skip_ref),
        (tw_hbm, twiddle), (dft_hbm, dft), (w_hbm, w_in),
    ]
    local = [pltpu.make_async_copy(source, target, local_sem.at[i]) for i, (source, target) in enumerate(pairs)]
    for copy in local:
        copy.start()

    for i in range(3):
        local[i].wait()
    ends = [x[112:128, :].astype(F32)[14:16, :] for x in (k_in, v_in)]
    tails[...] = jnp.concatenate(ends, axis=0).astype(BF16)
    for i in range(3, 6):
        local[i].wait()

    def turned(block):
        return block.astype(BF16).T.reshape(TILES, ROWS, LANES)

    def place(i):
        return i * 128 // WIDTH, pl.ds(lax.rem(i * 128, WIDTH) // ROWS, TILES)

    def turn(i, carry):
        cols = pl.ds(pl.multiple_of(i * 128, 128), 128)
        part, blocks = place(i)
        h_send[part, blocks] = turned(h_in[:, cols])
        q_send[part, blocks] = turned(q_in[:, cols])
        return carry

    lax.fori_loop(0, 8, turn, 0)

    for i, x in enumerate((k_in, v_in)):

        def widen(r, carry):
            rows = pl.multiple_of(r * 16, 16)
            extended[i, pl.ds(rows + 8, 16), :] = x[pl.ds(rows, 16), :].astype(F32)
            return carry

        lax.fori_loop(0, 8, widen, 0)

    pl.semaphore_wait(barrier, n - 1 + 2)

    halo_copy = pltpu.make_async_remote_copy(
        src_ref=tails, dst_ref=halo, send_sem=halo_sem.at[0], recv_sem=halo_sem.at[1],
        device_id={"seq": lax.rem(me + 1, n)}, device_id_type=MESH,
    )
    halo_copy.start()

    def scatter(source, target, part, sems):
        for peer in peers:
            pltpu.make_async_remote_copy(
                src_ref=source.at[part, peer], dst_ref=target.at[part, me],
                send_sem=sems.at[0, part], recv_sem=sems.at[1, part],
                device_id={"seq": peer}, device_id_type=MESH,
            ).start()
        target[part, me] = source[part, me]

    def all_of(ref, part, sems):
        view = ref.at[part, pl.ds(0, BLOCKS - 1)]
        return pltpu.make_async_remote_copy(
            src_ref=view, dst_ref=view, send_sem=sems.at[0, part], recv_sem=sems.at[1, part],
            device_id={"seq": lax.rem(me + 1, n)}, device_id_type=MESH,
        )

    scatter(h_send, h_all, 0, h_sem)
    scatter(h_send, h_all, 1, h_sem)

    for i in range(8):
        cols = pl.ds(i * 128, 128)
        rows = jnp.concatenate([skip_ref[0:1, cols], fw_ref[0, :, cols], jnp.zeros((4, 128), F32)], axis=0)
        columns[cols, :] = rows.T

    halo_copy.wait()
    before = halo[...].astype(F32) * jnp.where(me == 0, 0.0, 1.0).astype(F32)
    for i in range(2):
        extended[i, 6:8, :] = before[2 * i : 2 * i + 2, :]

    def feature(i, cols):
        result = fw_ref[i + 1, 0:1, cols] * extended[i, 8:136, cols]
        result += fw_ref[i + 1, 1:2, cols] * extended[i, 7:135, cols]
        return result + fw_ref[i + 1, 2:3, cols] * extended[i, 6:134, cols]

    def gate(i, carry):
        cols = pl.ds(pl.multiple_of(i * 128, 128), 128)
        part, blocks = place(i)
        g_send[part, blocks] = turned(feature(0, cols) * feature(1, cols))
        return carry

    for part in range(PARTS):
        lax.fori_loop(part * (8 // PARTS), (part + 1) * (8 // PARTS), gate, 0, unroll=True)
        scatter(g_send, g_all, part, g_sem)
        scatter(q_send, q_all, part, q_sem)

    local[6].wait()
    local[7].wait()

    def filters(part, carry):
        all_of(h_all, part, h_sem).wait_recv()
        forward_blocks(h_all, part, mid, high_ref, low_ref, twiddle)
        filter_spectrum(high_ref, low_ref, dft, h_spec, part)
        return carry

    lax.fori_loop(0, PARTS, filters, 0)

    lane = lax.broadcasted_iota(jnp.int32, (ROWS, LANES), 1)

    def query_features(part):
        own = columns[pl.ds(pl.multiple_of(part * WIDTH + me * ROWS, ROWS), ROWS), :]
        w0, w1, w2 = [jnp.broadcast_to(own[:, i : i + 1], (ROWS, LANES)) for i in range(1, 4)]
        gains[...] = jnp.broadcast_to(own[:, 0:1], (ROWS, LANES))
        before1 = before2 = jnp.zeros((ROWS, LANES), F32)
        for k in range(BLOCKS):
            x = q_all[part, k].astype(F32)
            now1, now2 = pltpu.roll(x, 1, 1), pltpu.roll(x, 2, 1)
            shifted = w1 * jnp.where(lane < 1, before1, now1) + w2 * jnp.where(lane < 2, before2, now2)
            feature_q[k] = w0 * x + shifted
            before1, before2 = now1, now2

    def convolve(part, carry):
        all_of(g_all, part, g_sem).wait_recv()
        forward_blocks(g_all, part, mid, high_ref, low_ref, twiddle)
        multiply_spectra(high_ref, low_ref, dft, h_spec, part, v_spec)
        all_of(q_all, part, q_sem).wait_recv()
        query_features(part)
        inverse_blocks(v_spec, mid, m_send, part, twiddle, feature_q, gains, g_all)
        for side, target in ((1, across), (0, mine)):
            for peer in peers + [me] * side:
                pltpu.make_async_remote_copy(
                    src_ref=m_send.at[part, peer], dst_ref=mixed.at[mine, part, me],
                    send_sem=m_sem.at[0, side, part], recv_sem=m_sem.at[1, side, part],
                    device_id={"seq": peer, "ch": target}, device_id_type=MESH,
                ).start()
        mixed[mine, part, me] = m_send[part, me]
        return carry

    lax.fori_loop(0, PARTS, convolve, 0)

    def arrived(side, part):
        view = mixed.at[0, part, pl.ds(0, BLOCKS - 1 + side)]
        return pltpu.make_async_remote_copy(
            src_ref=view, dst_ref=view, send_sem=m_sem.at[0, side, part], recv_sem=m_sem.at[1, side, part],
            device_id={"ch": across}, device_id_type=MESH,
        )

    def swap(slot, side, part):
        return pltpu.make_async_remote_copy(
            src_ref=mixed.at[slot, part], dst_ref=mixed.at[slot, part],
            send_sem=swap_sem.at[0, side, part], recv_sem=swap_sem.at[1, side, part],
            device_id={"ch": beside}, device_id_type=MESH,
        )

    def product(tokens, slot, part, cols):
        rows = pl.ds(pl.multiple_of(slot * 1024 + part * WIDTH, WIDTH), WIDTH)
        return dot(tokens, w_in[rows, cols])

    def by_token(slot, part):
        return mixed[slot, part].reshape(WIDTH, LANES).T

    def project(slot, part):
        tokens = by_token(slot, part)

        for j in range(4):
            cols = pl.ds(j * 256, 256)
            total[:, cols] = total[:, cols] + product(tokens, slot, part, cols)

    total[...] = jnp.zeros_like(total)
    local[8].wait()
    for part in range(PARTS):
        arrived(1, part).wait_recv()
        swap(across, 1, part).start()
        project(across, part)
        arrived(0, part).wait_recv()
        swap(mine, 0, part).start()
        project(mine, part)
        swap(diagonal, 1, part).wait_recv()
        project(diagonal, part)
        swap(beside, 0, part).wait_recv()
        if part < PARTS - 1:
            project(beside, part)
    tokens = by_token(beside, PARTS - 1)

    def finish(j):
        cols = pl.ds(j * 256, 256)
        return pltpu.make_async_copy(out_stage.at[:, cols], out_ref.at[:, cols], out_sem.at[j])

    for j in range(4):
        cols = pl.ds(j * 256, 256)
        out_stage[:, cols] = (total[:, cols] + product(tokens, beside, PARTS - 1, cols)).astype(BF16)
        finish(j).start()

    for part in range(PARTS):
        all_of(h_all, part, h_sem).wait_send()
        all_of(g_all, part, g_sem).wait_send()
        all_of(q_all, part, q_sem).wait_send()
        for side in range(2):
            arrived(side, part).wait_send()
            swap(mine, side, part).wait_send()
    for j in range(4):
        finish(j).wait()


def shards(query_proj, key_proj, value_proj, feat_weight, long_filter, skip_gain, out_weight):
    twiddle, dft = tables()
    anywhere = pl.BlockSpec(memory_space=pl.ANY)
    tokens, channels = query_proj.shape
    spectrum = (SPECTRUM_ROWS, 2 * LANES)
    turned = (PARTS, BLOCKS, ROWS, LANES)
    return pl.pallas_call(
        kernel,
        out_shape=jax.ShapeDtypeStruct((tokens, channels), BF16),
        in_specs=[anywhere] * 9,
        out_specs=anywhere,
        scratch_shapes=[
            pltpu.VMEM((tokens, channels), BF16),
            pltpu.VMEM((tokens, channels), BF16),
            pltpu.VMEM((tokens, channels), BF16),
            pltpu.VMEM(feat_weight.shape, F32),
            pltpu.VMEM((tokens, channels), F32),
            pltpu.VMEM((1, channels), F32),
            pltpu.VMEM(out_weight.shape, BF16),
            pltpu.VMEM(twiddle.shape, F32),
            pltpu.VMEM(dft.shape, BF16),
            pltpu.VMEM((4, channels), BF16),
            pltpu.VMEM((4, channels), BF16),
            pltpu.VMEM((2, tokens + 8, channels), F32),
            pltpu.VMEM((channels, 8), F32),
            pltpu.VMEM((BLOCKS, ROWS, LANES), F32),
            pltpu.VMEM((ROWS, LANES), F32),
            pltpu.VMEM(turned, BF16),
            pltpu.VMEM(turned, BF16),
            pltpu.VMEM(turned, BF16),
            pltpu.VMEM(turned, BF16),
            pltpu.VMEM(turned, BF16),
            pltpu.VMEM(turned, BF16),
            pltpu.VMEM(turned, BF16),
            pltpu.VMEM((2, 4, 8, ROWS, LANES), F32),
            pltpu.VMEM(spectrum, BF16),
            pltpu.VMEM(spectrum, BF16),
            pltpu.VMEM((PARTS,) + spectrum, F32),
            pltpu.VMEM(spectrum, F32),
            pltpu.VMEM((4,) + turned, BF16),
            pltpu.VMEM((tokens, channels), F32),
            pltpu.VMEM((tokens, channels), BF16),
            pltpu.SemaphoreType.DMA((9,)),
            pltpu.SemaphoreType.DMA((2,)),
            pltpu.SemaphoreType.DMA((2, PARTS)),
            pltpu.SemaphoreType.DMA((2, PARTS)),
            pltpu.SemaphoreType.DMA((2, PARTS)),
            pltpu.SemaphoreType.DMA((2, 2, PARTS)),
            pltpu.SemaphoreType.DMA((2, 2, PARTS)),
            pltpu.SemaphoreType.DMA((4,)),
        ],
        compiler_params=pltpu.CompilerParams(
            collective_id=0, has_side_effects=True, vmem_limit_bytes=56 * 1024 * 1024
        ),
        name="mixer",
    )(
        query_proj, key_proj, value_proj, feat_weight, long_filter, skip_gain[None, :], out_weight, twiddle, dft,
    )


def solution(mesh):
    placed = (
        P("seq", "ch"),
        P("seq", "ch"),
        P("seq", "ch"),
        P(None, None, "ch"),
        P("seq", "ch"),
        P("ch"),
        P(None, "ch"),
    )
    return jax.shard_map(shards, mesh=mesh, in_specs=placed, out_specs=P("seq", "ch"), check_vma=False)
```
